256 devices in a mesh: seq: 64 (over x, z, core), tensor: 4 (over y).
Axes of the slice: x: 4, y: 4, z: 8, core: 2. Of those that a mesh axis runs over, the one named last changes fastest.
Arguments:
- queries: bfloat16 [32768, 16384], P(('seq', 'tensor')), may hold values from -200 to 200
- keys: bfloat16 [32768, 1024], P(('seq', 'tensor')), may hold values from -6 to 6
- values: bfloat16 [32768, 1024], P(('seq', 'tensor')), may hold values from -6 to 6
- lengths: int32 [48], replicated, may hold values from 1 to 7, 256 in all
- parents: int32 [48], replicated, may hold values from 0 to 46, as said below
- headers: int32 [48], replicated, may hold values from 1 to 2
Outputs:
- attention: bfloat16 [32768, 16384], P(('seq', 'tensor'))
The draws below stay inside these ranges and needn't reach their ends.
Inputs may be any that keep to these rules, and one draw needn't show every extreme that they name: parents[0] is 0, the root; every other child c has parents[c] < c; from every child the root is reached in at most 3 steps, and some child needs exactly 3.
All inputs are finite; a program needn't handle non-finite values.
Results may differ from the reference program's by a relative error of at most 0.0055.
Values may be sent and summed in bfloat16 or wider, within the bound.
No kernel may reach another device: no remote copies, remote signals or barrier semaphores. Data moves between devices by JAX's collectives and lax.ppermute only.
A program may use at most 128 MiB of HBM per device.

```python
import math
import jax
import jax.numpy as jnp
import numpy as np
from jax import lax

QUERY_HEAD_COUNT = 128
KEY_VALUE_HEADS = 8
HEAD_SIZE = 128
MASK_BLOCK_SIZE = 128
MAXLEN = 7
HDR = 2
DEPTH = 4
WINDOW_TOKENS = 32768
MASK_BLOCKS = 256
NC = 48


def shared_fields(key):
    key_value_start = jax.random.truncated_normal(jax.random.fold_in(key, 11), -6.0, 6.0, (WINDOW_TOKENS, KEY_VALUE_HEADS * HEAD_SIZE), jnp.float32)
    query_base = jax.random.truncated_normal(jax.random.fold_in(key, 12), -6.0, 6.0, (WINDOW_TOKENS, QUERY_HEAD_COUNT * HEAD_SIZE), jnp.float32)
    return (query_base, key_value_start)


def draw_queries(key, part):
    query_base, key_value_start = shared_fields(key)
    return query_base.astype(jnp.bfloat16)


def draw_keys(key, part):
    query_base, key_value_start = shared_fields(key)
    return key_value_start.astype(jnp.bfloat16)


def draw_parents(key, part):
    child_ids = jnp.arange(NC, dtype=jnp.int32)
    drawn = jax.random.randint(jax.random.fold_in(key, 21), (NC,), 1, DEPTH - 1, dtype=jnp.int32)
    levels = jnp.where(child_ids <= DEPTH - 3, child_ids, drawn)
    levels = jnp.where(child_ids == NC - 2, DEPTH - 2, levels)
    levels = jnp.where(child_ids == NC - 1, DEPTH - 1, levels)
    wanted = levels - 1
    scores = jax.random.randint(jax.random.fold_in(key, 22), (NC, NC), 0, 1024, dtype=jnp.int32) * NC + child_ids[None, :]
    earlier = (child_ids[None, :] < child_ids[:, None]) & (levels[None, :] == wanted[:, None])
    best = jnp.max(jnp.where(earlier, scores, -1), axis=1)
    parent_ids = jnp.where(best >= 0, best % NC, 0)
    parent_ids = jnp.where(child_ids == NC - 1, NC - 2, parent_ids)
    parent_ids = jnp.where(child_ids == 0, 0, parent_ids)
    return parent_ids.astype(jnp.int32)


def with_ends(values, rng, low, top_value):
    index_at = [jax.random.randint(jax.random.fold_in(rng, axis), (), 0, length) for axis, length in enumerate(values.shape)]
    main_axis = values.shape.index(max(values.shape))
    beside = index_at[:main_axis] + [(index_at[main_axis] + 1) % values.shape[main_axis]] + index_at[main_axis + 1:]
    return values.at[tuple(index_at)].set(low).at[tuple(beside)].set(top_value)


def shard_levels(own_key, shape, cuts, smallest, largest):
    def one(position, shards_of):
        steps = jax.random.uniform(jax.random.fold_in(jax.random.fold_in(own_key, 6), position), (shards_of,), jnp.float32, smallest / len(cuts), largest / len(cuts))
        return jnp.repeat(jnp.exp(steps), shape[position] // shards_of).reshape((-1,) + (1,) * (len(shape) - position - 1))

    factor_of = one(*cuts[0])
    for cut in cuts[1:]:
        factor_of = factor_of * one(*cut)
    return factor_of


def profile(amount, total, bound, lean):
    portions = [(1 << 20) // math.isqrt(standing ** lean) + 1 for standing in range(2, amount + 1)]
    rest, given = total - bound - (amount - 1), [1] * (amount - 1)
    while rest > 0:
        candidates = [i for i in range(amount - 1) if given[i] < bound]
        mass, budget = sum([portions[i] for i in candidates]), rest
        for i in candidates:
            extra = min(bound - given[i], max(1, budget * portions[i] // mass), rest)
            given[i] = given[i] + extra
            rest = rest - extra
    return np.array([bound] + given)


def ragged_sizes(rng, count, total, most, slope):
    if count == 2:
        one = jax.random.randint(rng, (), max(1, total - most), min(most, total - 1) + 1)
        return jnp.stack([one, total - one])
    sizes = jnp.asarray(profile(count, total, most, slope), jnp.int32)
    pairs = (count - 1) // 2
    donor, taker = sizes[1:1 + 2 * pairs:2], sizes[2:2 + 2 * pairs:2]
    slack = jnp.minimum(donor - 1, most - taker)
    shifted = jax.random.randint(jax.random.fold_in(rng, 1), (pairs,), 0, 1 << 20) % (slack + 1)
    sizes = sizes.at[1:1 + 2 * pairs:2].set(donor - shifted).at[2:2 + 2 * pairs:2].set(taker + shifted)
    return sizes[jax.random.permutation(jax.random.fold_in(rng, 2), count)]


def gaussian(key, shape, spread, bound, cuts=(), held_as=jnp.bfloat16):
    values = spread * jax.random.normal(key, shape, jnp.float32)
    if cuts:
        values = values * shard_levels(key, shape, cuts, -0.22, 0.18)
    return jnp.clip(values, -bound, bound).astype(held_as)


def setup_inputs(seed: int = 0) -> dict:
    splits = jax.random.split(jax.random.key(seed), 7)
    return {
        "queries": draw_queries(jax.random.fold_in(splits[6], 71), 0),
        "keys": draw_keys(jax.random.fold_in(splits[6], 71), 0),
        "values": gaussian(splits[2], (WINDOW_TOKENS, KEY_VALUE_HEADS * HEAD_SIZE), 1.0, 6.0, ((0, 256),)),
        "lengths": ragged_sizes(splits[3], NC, MASK_BLOCKS, MAXLEN, 1).astype(jnp.int32),
        "parents": draw_parents(jax.random.fold_in(splits[6], 71), 0),
        "headers": with_ends(jax.random.randint(splits[5], (NC,), 1, HDR + 1), jax.random.fold_in(splits[5], 1), 1, HDR).astype(jnp.int32),
    }


def lookup(small_table, where_ids):
    slot_ids = jnp.arange(small_table.shape[0], dtype=jnp.int32)
    picked = jnp.where(where_ids[..., None] == slot_ids, small_table, 0)
    return jnp.sum(picked, axis=-1).astype(jnp.int32)


def block_lists(lengths, parents, headers, block_ids):
    starts = (jnp.cumsum(lengths) - lengths).astype(jnp.int32)
    header_len = jnp.minimum(headers, lengths).astype(jnp.int32)
    owner_child = (jnp.sum((starts[None, :] <= block_ids[:, None]).astype(jnp.int32), axis=1) - 1).astype(jnp.int32)
    entry_list = []
    flag_list = []
    current = owner_child
    for level_step in range(DEPTH - 1):
        has_parent = current != 0
        current = lookup(parents, current)
        first_block = lookup(starts, current)
        header_count = lookup(header_len, current)
        for offset in range(HDR):
            entry_list.append(first_block + offset)
            flag_list.append(has_parent & (offset < header_count))
    first_block = lookup(starts, owner_child)
    for offset in range(MAXLEN):
        entry_list.append(first_block + offset)
        flag_list.append(first_block + offset <= block_ids)
    entries = jnp.stack(entry_list, axis=1)
    flags = jnp.stack(flag_list, axis=1)
    entries = jnp.where(flags, entries, 0).astype(jnp.int32)
    return entries, flags


def reference(queries, keys, values, lengths, parents, headers):
    block_ids = jnp.arange(MASK_BLOCKS, dtype=jnp.int32)
    entries, flags = block_lists(lengths, parents, headers, block_ids)
    query_group_width = QUERY_HEAD_COUNT // KEY_VALUE_HEADS
    blocked_queries = queries.reshape(MASK_BLOCKS, MASK_BLOCK_SIZE, KEY_VALUE_HEADS, query_group_width, HEAD_SIZE)
    blocked_keys = keys.reshape(MASK_BLOCKS, MASK_BLOCK_SIZE, KEY_VALUE_HEADS, HEAD_SIZE)
    blocked_values = values.reshape(MASK_BLOCKS, MASK_BLOCK_SIZE, KEY_VALUE_HEADS, HEAD_SIZE)
    positions = jnp.arange(MASK_BLOCK_SIZE, dtype=jnp.int32)
    causal = positions[None, :] <= positions[:, None]
    score_scale = HEAD_SIZE ** -0.5

    def attend(record):
        query_block, entry_row, flag_row, block_id = record
        key_tile = jnp.take(blocked_keys, entry_row, axis=0)
        value_tile = jnp.take(blocked_values, entry_row, axis=0)
        scores = jnp.einsum('thgd,kshd->hgtks', query_block.astype(jnp.float32), key_tile.astype(jnp.float32)) * score_scale
        usable = flag_row[None, :, None] & ((entry_row[None, :, None] != block_id) | causal[:, None, :])
        scores = jnp.where(usable[None, None], scores, -jnp.inf)
        row_max = jnp.max(scores, axis=(3, 4))
        weights = jnp.exp(scores - row_max[..., None, None])
        weight_sum = jnp.sum(weights, axis=(3, 4))
        rounded = lax.optimization_barrier(weights.astype(jnp.bfloat16))
        mixed = jnp.einsum('hgtks,kshd->thgd', rounded.astype(jnp.float32), value_tile.astype(jnp.float32))
        result = mixed / jnp.transpose(weight_sum, (2, 0, 1))[..., None]
        return result.astype(jnp.bfloat16).reshape(MASK_BLOCK_SIZE, QUERY_HEAD_COUNT * HEAD_SIZE)

    output = lax.map(attend, (blocked_queries, entries, flags, block_ids))
    return output.reshape(WINDOW_TOKENS, QUERY_HEAD_COUNT * HEAD_SIZE)
```

```python
import functools

import jax
import jax.numpy as jnp
from jax import lax
from jax.experimental import pallas as pl
from jax.experimental.pallas import tpu as pltpu
from jax.sharding import Mesh
from jax.sharding import PartitionSpec as P

HEAD = 128
BLK = 128
MAXLEN = 7
HDR = 2
DEPTH = 4
GROUP = 8
WINDOW = MAXLEN - 1
NEAR = WINDOW + GROUP
FAST_SLOTS = 32
ALL_SLOTS = 64
LIST = WINDOW + (DEPTH - 1) * HDR
NEG = -1e30
EXP_SCALE = HEAD ** (-0.5) * 1.4426950408889634


def lookup(table, ids):
    slots = jnp.arange(table.shape[0], dtype=jnp.int32)
    return jnp.sum(jnp.where(ids[..., None] == slots, table, 0), axis=-1)


def tree_tables(lengths, parents, headers, group_id):
    child_count = lengths.shape[0]
    child = jnp.arange(child_count, dtype=jnp.int32)
    before = child[None, :] < child[:, None]
    starts = jnp.sum(jnp.where(before, lengths[None, :], 0), axis=1)
    header_len = jnp.minimum(headers, lengths)
    inner = jnp.any((parents[None, :] == child[:, None]) & (child[None, :] > 0), axis=1)
    kept = jnp.where(inner, header_len, 0)
    slot_of = jnp.sum(jnp.where(before, kept[None, :], 0), axis=1)
    total = jnp.sum(kept)
    slot = jnp.arange(ALL_SLOTS, dtype=jnp.int32)
    inside = (slot[:, None] >= slot_of[None, :]) & (slot[:, None] < (slot_of + kept)[None, :])
    slot_block = jnp.sum(
        jnp.where(inside, starts[None, :] + slot[:, None] - slot_of[None, :] + 1, 0), axis=1
    ) - 1

    block = group_id * GROUP + jnp.arange(GROUP, dtype=jnp.int32)
    owner = jnp.sum((starts[None, :] <= block[:, None]).astype(jnp.int32), axis=1) - 1
    start = lookup(starts, owner)
    own_full = block - start
    k = jnp.arange(LIST, dtype=jnp.int32)[None, :]
    entries = jnp.where(k < own_full[:, None], (start - group_id * GROUP + WINDOW)[:, None] + k, 0)
    filled = own_full
    current = owner
    for _ in range(DEPTH - 1):
        has_parent = current != 0
        current = lookup(parents, current)
        count = jnp.where(has_parent, lookup(header_len, current), 0)
        first = NEAR + lookup(slot_of, current)
        here = (k >= filled[:, None]) & (k < (filled + count)[:, None])
        entries = jnp.where(here, first[:, None] + k - filled[:, None], entries)
        filled = filled + count
    return slot_block, total, entries, filled


def attend_kernel(heads, filled_ref, entries_ref, near_ref, fast_ref, rest_ref, query_ref, out_ref,
                  pool, sems, scores, top, acc, den):
    step = pl.program_id(0)
    rows = heads * BLK

    @pl.when(step == 0)
    def _():
        copies = [
            pltpu.make_async_copy(near_ref, pool.at[pl.ds(0, NEAR)], sems.at[0]),
            pltpu.make_async_copy(fast_ref, pool.at[pl.ds(NEAR, FAST_SLOTS)], sems.at[1]),
            pltpu.make_async_copy(
                rest_ref, pool.at[pl.ds(NEAR + FAST_SLOTS, ALL_SLOTS - FAST_SLOTS)], sems.at[2]
            ),
        ]
        for c in copies:
            c.start()
        for c in copies:
            c.wait()

    filled = filled_ref[step]
    pairs = filled // 2
    odd = filled - 2 * pairs
    last = entries_ref[step, jnp.maximum(filled - 1, 0)]
    diagonal = step + WINDOW

    def tile(which, a, b):
        return jnp.concatenate([pool[a, which], pool[b, which]], axis=0)

    def queries(h):
        return query_ref[0, :, h * HEAD:(h + 1) * HEAD]

    def score(q, keys):
        return lax.dot_general(q, keys, (((1,), (1,)), ((), ())), preferred_element_type=jnp.float32)

    row = lax.broadcasted_iota(jnp.int32, (BLK, 2 * BLK), 0)
    col = lax.broadcasted_iota(jnp.int32, (BLK, 2 * BLK), 1)
    usable = (col <= row) | ((col >= BLK) & (odd == 1))
    keys = tile(0, diagonal, last)
    for h in range(heads):
        s = jnp.where(usable, score(queries(h), keys), NEG)
        r = slice(h * BLK, (h + 1) * BLK)
        scores[0, r, :] = s
        top[r, :] = jnp.maximum(s[:, :BLK], s[:, BLK:])

    def first_pass(p, carry):
        keys = tile(0, entries_ref[step, 2 * p], entries_ref[step, 2 * p + 1])
        for h in range(heads):
            s = score(queries(h), keys)
            r = slice(h * BLK, (h + 1) * BLK)
            scores[p + 1, r, :] = s
            top[r, :] = jnp.maximum(top[r, :], jnp.maximum(s[:, :BLK], s[:, BLK:]))
        return carry

    lax.fori_loop(0, pairs, first_pass, 0)

    def weigh(p, a, b, fresh):
        vals = tile(1, a, b)
        for h in range(heads):
            r = slice(h * BLK, (h + 1) * BLK)
            t = top[r, :]
            s = scores[p, r, :]
            w0 = jnp.exp2((s[:, :BLK] - t) * EXP_SCALE)
            w1 = jnp.exp2((s[:, BLK:] - t) * EXP_SCALE)
            mixed = jnp.dot(
                jnp.concatenate([w0, w1], axis=1).astype(jnp.bfloat16), vals,
                preferred_element_type=jnp.float32,
            )
            if fresh:
                den[r, :] = w0 + w1
                acc[r, :] = mixed
            else:
                den[r, :] += w0 + w1
                acc[r, :] += mixed

    for h in range(heads):
        r = slice(h * BLK, (h + 1) * BLK)
        top[r, :] = jnp.broadcast_to(jnp.max(top[r, :], axis=1, keepdims=True), (BLK, BLK))
    weigh(0, diagonal, last, True)

    def second_pass(p, carry):
        weigh(p + 1, entries_ref[step, 2 * p], entries_ref[step, 2 * p + 1], False)
        return carry

    lax.fori_loop(0, pairs, second_pass, 0)
    for h in range(heads):
        r = slice(h * BLK, (h + 1) * BLK)
        total = jnp.sum(den[r, :], axis=1, keepdims=True)
        out_ref[0, :, h * HEAD:(h + 1) * HEAD] = (acc[r, :] / total).astype(out_ref.dtype)


def attend(filled, entries, near, fast, rest, query):
    width = query.shape[2]
    heads = width // HEAD
    rows = heads * BLK
    longest = 1 + LIST // 2
    return pl.pallas_call(
        functools.partial(attend_kernel, heads),
        out_shape=jax.ShapeDtypeStruct(query.shape, query.dtype),
        grid_spec=pltpu.PrefetchScalarGridSpec(
            num_scalar_prefetch=2,
            grid=(GROUP,),
            in_specs=[
                pl.BlockSpec(memory_space=pl.ANY),
                pl.BlockSpec(memory_space=pl.ANY),
                pl.BlockSpec(memory_space=pl.ANY),
                pl.BlockSpec((1, BLK, width), lambda i, *_: (i, 0, 0)),
            ],
            out_specs=pl.BlockSpec((1, BLK, width), lambda i, *_: (i, 0, 0)),
            scratch_shapes=[
                pltpu.VMEM((NEAR + ALL_SLOTS, 2, BLK, HEAD), jnp.bfloat16),
                pltpu.SemaphoreType.DMA((3,)),
                pltpu.VMEM((longest, rows, 2 * BLK), jnp.float32),
                pltpu.VMEM((rows, BLK), jnp.float32),
                pltpu.VMEM((rows, HEAD), jnp.float32),
                pltpu.VMEM((rows, BLK), jnp.float32),
            ],
        ),
        compiler_params=pltpu.CompilerParams(vmem_limit_bytes=60 * 1024 * 1024),
        name="attend",
    )(filled, entries, near, fast, rest, query)


def body(queries, keys, values, lengths, parents, headers):
    group_id = lax.axis_index(("x", "z"))
    groups = lax.axis_size(("x", "z"))
    inside = ("c", "t")
    across = ("x", "z")
    slot_block, total, entries, filled = tree_tables(lengths, parents, headers, group_id)

    def split_heads(a):
        return jnp.transpose(a.reshape(BLK, GROUP, HEAD), (1, 0, 2))

    own = jnp.stack([split_heads(keys), split_heads(values)], axis=1)
    own = lax.all_to_all(own, inside, split_axis=0, concat_axis=0, tiled=True)
    before = lax.ppermute(own[GROUP - WINDOW:], across, [(j, j + 1) for j in range(groups - 1)])
    near = jnp.concatenate([before, own], axis=0)

    def gather_slots(first, count):
        blocks = slot_block[first:first + count]
        mine = blocks - group_id * GROUP
        picked = jnp.take(own, jnp.clip(mine, 0, GROUP - 1), axis=0)
        here = (mine >= 0) & (mine < GROUP)
        picked = jnp.where(here[:, None, None, None], picked, jnp.zeros((), own.dtype))
        return lax.psum(picked, across)

    fast = gather_slots(0, FAST_SLOTS)
    rest_count = ALL_SLOTS - FAST_SLOTS
    rest = lax.cond(
        total > FAST_SLOTS,
        lambda: gather_slots(FAST_SLOTS, rest_count),
        lambda: jnp.zeros((rest_count,) + own.shape[1:], own.dtype),
    )

    wide = jnp.transpose(queries.reshape(BLK, GROUP, -1), (1, 0, 2))
    mine = lax.all_to_all(wide, inside, split_axis=0, concat_axis=0, tiled=True)
    result = attend(filled, entries, near, fast, rest, mine)
    back = lax.all_to_all(result, inside, split_axis=0, concat_axis=0, tiled=True)
    return jnp.transpose(back, (1, 0, 2)).reshape(BLK, -1)


def solution(mesh):
    inner = Mesh(mesh.devices.reshape(4, 8, 2, 4), ("x", "z", "c", "t"))
    rows = P(("x", "z", "c", "t"), None)
    return jax.shard_map(
        body, mesh=inner, in_specs=(rows, rows, rows, P(), P(), P()), out_specs=rows, check_vma=False
    )
```

```python
import functools

import jax
import jax.numpy as jnp
from jax import lax
from jax.experimental import pallas as pl
from jax.experimental.pallas import tpu as pltpu
from jax.sharding import Mesh
from jax.sharding import PartitionSpec as P

HEAD = 128
BLK = 128
MAXLEN = 7
HDR = 2
DEPTH = 4
GROUP = 8
WINDOW = MAXLEN - 1
NEAR = 2 * GROUP
SLOTS = GROUP * (DEPTH - 2) * HDR + HDR
FAST_SLOTS = 8
REST_SLOTS = SLOTS - FAST_SLOTS
CHUNKS = 2
PACK_STEPS = 4
LIST = WINDOW + (DEPTH - 1) * HDR
NEG = -1e30
VMEM_LIMIT = 48 * 1024 * 1024
EXP_SCALE = HEAD ** (-0.5) * 1.4426950408889634


def lookup(table, ids):
    slots = jnp.arange(table.shape[0], dtype=jnp.int32)
    return jnp.sum(jnp.where(ids[..., None] == slots, table, 0), axis=-1)


def tree_tables(lengths, parents, headers, group_id, groups, order, place):
    child = jnp.arange(lengths.shape[0], dtype=jnp.int32)
    before = child[None, :] < child[:, None]
    starts = jnp.sum(jnp.where(before, lengths[None, :], 0), axis=1)
    header_len = jnp.minimum(headers, lengths)

    ancestor = jnp.zeros(before.shape, bool)
    climbed = child
    for _ in range(DEPTH - 1):
        has_parent = climbed != 0
        climbed = lookup(parents, climbed)
        ancestor |= has_parent[:, None] & (climbed[:, None] == child[None, :])

    first = jnp.arange(groups, dtype=jnp.int32)[:, None] * GROUP
    present = (starts[None, :] < first + GROUP) & ((starts + lengths)[None, :] > first)
    needed = jnp.any(present[:, :, None] & ancestor[None, :, :], axis=1)
    count = jnp.where(needed, header_len[None, :], 0)
    slot_of = jnp.sum(jnp.where(before[None, :, :], count[:, None, :], 0), axis=2)
    most = jnp.max(jnp.sum(count, axis=1))
    slot = jnp.arange(SLOTS, dtype=jnp.int32)[None, :, None]
    offset = slot - slot_of[:, None, :]
    inside = (offset >= 0) & (offset < count[:, None, :])
    slot_block = jnp.sum(jnp.where(inside, starts[None, None, :] + offset, 0), axis=2)

    block = group_id * GROUP + order
    owner = jnp.sum((starts[None, :] <= block[:, None]).astype(jnp.int32), axis=1) - 1
    start = lookup(starts, owner)
    filled = block - start
    my_slots = lax.dynamic_index_in_dim(slot_of, group_id, 0, keepdims=False)
    k = jnp.arange(LIST, dtype=jnp.int32)[None, :]
    near = (start - group_id * GROUP + GROUP)[:, None] + k
    half = near // GROUP
    near = half * GROUP + place(near - half * GROUP)
    entries = jnp.where(k < filled[:, None], near, 0)
    current = owner
    for _ in range(DEPTH - 1):
        has_parent = current != 0
        current = lookup(parents, current)
        size = jnp.where(has_parent, lookup(header_len, current), 0)
        at = NEAR + lookup(my_slots, current)
        here = (k >= filled[:, None]) & (k < (filled + size)[:, None])
        entries = jnp.where(here, at[:, None] + k - filled[:, None], entries)
        filled = filled + size
    return slot_block, most, entries, filled


def attend_kernel(chunk, filled_ref, entries_ref, order_ref, *refs):
    near_and_far, query_refs, refs = refs[:4], refs[4:4 + GROUP], refs[4 + GROUP:]
    out_ref, pool, asked, sems, query_sems, scores, top, acc, den = refs
    step = pl.program_id(0)
    rows = top.shape[0]
    heads = rows // BLK
    width = heads * HEAD

    def query_copy(n):
        return pltpu.make_async_copy(
            query_refs[n].at[:, pl.ds(chunk * width, width)], asked.at[n], query_sems.at[n]
        )

    @pl.when(step == 0)
    def _():
        copies = []
        at = 0
        for n, ref in enumerate(near_and_far):
            copies.append(pltpu.make_async_copy(ref, pool.at[pl.ds(at, ref.shape[0])], sems.at[n]))
            at += ref.shape[0]
        query_copy(0).start()
        for c in copies:
            c.start()
        for n in range(1, GROUP):
            query_copy(n).start()
        for c in copies:
            c.wait()

    for n in range(GROUP):
        @pl.when(step == n)
        def _():
            query_copy(n).wait()

    filled = filled_ref[step]
    pairs = filled // 2
    odd = filled - 2 * pairs
    last = entries_ref[step, jnp.maximum(filled - 1, 0)]
    diagonal = GROUP + step

    def tile(which, a, b):
        return jnp.concatenate([pool[a, which], pool[b, which]], axis=0)

    def queries(h):
        return asked[step, :, h * HEAD:(h + 1) * HEAD]

    def score(q, keys):
        return lax.dot_general(q, keys, (((1,), (1,)), ((), ())), preferred_element_type=jnp.float32)

    row = lax.broadcasted_iota(jnp.int32, (BLK, 2 * BLK), 0)
    col = lax.broadcasted_iota(jnp.int32, (BLK, 2 * BLK), 1)
    usable = (col <= row) | ((col >= BLK) & (odd == 1))
    keys = tile(0, diagonal, last)
    for h in range(heads):
        s = jnp.where(usable, score(queries(h), keys), NEG)
        r = slice(h * BLK, (h + 1) * BLK)
        scores[0, r, :] = s
        top[r, :] = jnp.maximum(s[:, :BLK], s[:, BLK:])

    def first_pass(p, carry):
        keys = tile(0, entries_ref[step, 2 * p], entries_ref[step, 2 * p + 1])
        for h in range(heads):
            s = score(queries(h), keys)
            r = slice(h * BLK, (h + 1) * BLK)
            scores[p + 1, r, :] = s
            top[r, :] = jnp.maximum(top[r, :], jnp.maximum(s[:, :BLK], s[:, BLK:]))
        return carry

    lax.fori_loop(0, pairs, first_pass, 0)

    def weigh(p, a, b, fresh):
        vals = tile(1, a, b)
        for h in range(heads):
            r = slice(h * BLK, (h + 1) * BLK)
            t = top[r, :]
            s = scores[p, r, :]
            w0 = jnp.exp2((s[:, :BLK] - t) * EXP_SCALE)
            w1 = jnp.exp2((s[:, BLK:] - t) * EXP_SCALE)
            mixed = jnp.dot(
                jnp.concatenate([w0, w1], axis=1).astype(jnp.bfloat16), vals,
                preferred_element_type=jnp.float32,
            )
            if fresh:
                den[r, :] = w0 + w1
                acc[r, :] = mixed
            else:
                den[r, :] += w0 + w1
                acc[r, :] += mixed

    for h in range(heads):
        r = slice(h * BLK, (h + 1) * BLK)
        top[r, :] = jnp.broadcast_to(jnp.max(top[r, :], axis=1, keepdims=True), (BLK, BLK))
    weigh(0, diagonal, last, True)

    def second_pass(p, carry):
        weigh(p + 1, entries_ref[step, 2 * p], entries_ref[step, 2 * p + 1], False)
        return carry

    lax.fori_loop(0, pairs, second_pass, 0)
    for h in range(heads):
        r = slice(h * BLK, (h + 1) * BLK)
        total = jnp.sum(den[r, :], axis=1, keepdims=True)
        out_ref[0, :, h * HEAD:(h + 1) * HEAD] = (acc[r, :] / total).astype(out_ref.dtype)


def copy_kernel(*refs):
    *sources, out_ref = refs
    at = 0
    for ref in sources:
        piece = ref[...].reshape(BLK, -1)
        width = piece.shape[1]
        if out_ref.ndim == 3:
            out_ref[0, :, at:at + width] = piece
        else:
            out_ref[:, at:at + width] = piece
        at += width


def pack_kernel(target_ref, query_ref, *out_refs):
    width = out_refs[0].shape[1]
    for n, out_ref in enumerate(out_refs):
        out_ref[...] = query_ref[:, pl.ds(pl.multiple_of(target_ref[n] * width, width), width)]


def pack(targets, queries):
    total = queries.shape[1]
    width = total // GROUP
    return pl.pallas_call(
        pack_kernel,
        out_shape=[jax.ShapeDtypeStruct((BLK, width), queries.dtype)] * GROUP,
        grid_spec=pltpu.PrefetchScalarGridSpec(
            num_scalar_prefetch=1,
            grid=(PACK_STEPS,),
            in_specs=[pl.BlockSpec((BLK // PACK_STEPS, total), lambda i, *_: (i, 0))],
            out_specs=[pl.BlockSpec((BLK // PACK_STEPS, width), lambda i, *_: (i, 0))] * GROUP,
        ),
        cost_estimate=pl.CostEstimate(flops=0, bytes_accessed=4 * BLK * total, transcendentals=0),
        name="pack",
    )(targets, queries)


def unpack(parts):
    width = parts[0].shape[2]
    total = GROUP * CHUNKS * width
    return pl.pallas_call(
        copy_kernel,
        out_shape=jax.ShapeDtypeStruct((BLK, total), parts[0].dtype),
        grid=(GROUP,),
        in_specs=[pl.BlockSpec((1, BLK, width), lambda i: (i, 0, 0))] * CHUNKS,
        out_specs=pl.BlockSpec((BLK, CHUNKS * width), lambda i: (0, i)),
        cost_estimate=pl.CostEstimate(flops=0, bytes_accessed=4 * BLK * total, transcendentals=0),
        name="unpack",
    )(*parts)


def attend(filled, entries, order, before, own, fast, rest, query, chunk):
    width = query[0].shape[1] // CHUNKS
    rows = width // HEAD * BLK
    longest = 1 + LIST // 2
    return pl.pallas_call(
        functools.partial(attend_kernel, chunk),
        out_shape=jax.ShapeDtypeStruct((GROUP, BLK, width), query[0].dtype),
        grid_spec=pltpu.PrefetchScalarGridSpec(
            num_scalar_prefetch=3,
            grid=(GROUP,),
            in_specs=[pl.BlockSpec(memory_space=pl.ANY)] * (4 + GROUP),
            out_specs=pl.BlockSpec((1, BLK, width), lambda i, f, e, order_ref: (order_ref[i], 0, 0)),
            scratch_shapes=[
                pltpu.VMEM((NEAR + SLOTS, 2, BLK, HEAD), jnp.bfloat16),
                pltpu.VMEM((GROUP, BLK, width), jnp.bfloat16),
                pltpu.SemaphoreType.DMA((4,)),
                pltpu.SemaphoreType.DMA((GROUP,)),
                pltpu.VMEM((longest, rows, 2 * BLK), jnp.float32),
                pltpu.VMEM((rows, BLK), jnp.float32),
                pltpu.VMEM((rows, HEAD), jnp.float32),
                pltpu.VMEM((rows, BLK), jnp.float32),
            ],
        ),
        compiler_params=pltpu.CompilerParams(vmem_limit_bytes=VMEM_LIMIT),
        cost_estimate=pl.CostEstimate(
            flops=GROUP * rows * 4 * 8 * BLK * HEAD, bytes_accessed=6 << 20, transcendentals=0
        ),
        name="attend",
    )(filled, entries, order, before, own, fast, rest, *query)


def body(queries, keys, values, lengths, parents, headers):
    inside = ("c", "t")
    across = ("x", "z")
    group_id = lax.axis_index(across)
    groups = lax.axis_size(across)
    pieces = 2 * BLK // groups

    def tiles(a):
        return jnp.transpose(a.reshape(-1, pieces, GROUP, HEAD), (0, 2, 1, 3))

    def exchange(a):
        return lax.all_to_all(a, inside, split_axis=0, concat_axis=0, tiled=True)

    sent = jnp.concatenate([tiles(keys), tiles(values)], axis=0)
    everyone = lax.all_to_all(sent.reshape(-1, pieces, HEAD), across + inside, split_axis=0, concat_axis=0, tiled=True)
    core = lax.axis_index("c")
    ring = lax.axis_index("t")
    ring_size = lax.axis_size("t")
    core_size = lax.axis_size("c")
    moves = [(dc, dt) for dc in range(core_size) for dt in range(ring_size)]

    def place(r):
        return (core ^ (r // ring_size)) * ring_size + (ring - r % ring_size) % ring_size

    def move(piece, dc, dt):
        pairs = [
            (c * ring_size + t, (c ^ dc) * ring_size + (t + dt) % ring_size)
            for c in range(core_size)
            for t in range(ring_size)
        ]
        return lax.ppermute(piece, inside, pairs)

    def indices(sign):
        return jnp.stack([(core ^ dc) * ring_size + (ring + sign * dt) % ring_size for dc, dt in moves])

    targets = indices(1)
    order = indices(-1)
    packed = pack(targets, queries)
    mine = []
    for n, (dc, dt) in enumerate(moves):
        piece = packed[n]
        if dt == 2:
            hop = 1 - 2 * dc
            piece = move(piece, 0, hop)
            piece = move(piece, dc, hop)
        elif dc or dt:
            piece = move(piece, dc, dt)
        mine.append(piece)

    slot_block, most, entries, filled = tree_tables(lengths, parents, headers, group_id, groups, order, place)
    blocks = (-1, 2, BLK, HEAD)
    own = []
    for n, (dc, dt) in enumerate(moves):
        piece = lax.dynamic_index_in_dim(sent, targets[n], 1, keepdims=False)
        own.append(move(piece, dc, dt) if dc or dt else piece)
    own = jnp.stack(own).reshape(blocks)
    before = lax.ppermute(own, across, [(j, j + 1) for j in range(groups - 1)])

    def fetch(first, count):
        wanted = slot_block[:, first:first + count].reshape(-1)
        picked = jnp.take(everyone, wanted, axis=0, mode="clip").reshape(groups, count, pieces, HEAD)
        got = lax.all_to_all(picked, across, split_axis=0, concat_axis=0, tiled=True)
        return jnp.transpose(got, (1, 0, 2, 3)).reshape(blocks)

    fast = fetch(0, FAST_SLOTS)
    rest = lax.cond(
        most > FAST_SLOTS,
        lambda: fetch(FAST_SLOTS, REST_SLOTS),
        lambda: jnp.zeros((REST_SLOTS,) + own.shape[1:], own.dtype),
    )

    parts = []
    for chunk in range(CHUNKS):
        parts.append(exchange(attend(filled, entries, order, before, own, fast, rest, mine, chunk)))
    return unpack(parts)


def solution(mesh):
    inner = Mesh(mesh.devices.reshape(4, 8, 2, 4), ("x", "z", "c", "t"))
    rows = P(("x", "z", "c", "t"), None)
    return jax.shard_map(body, mesh=inner, in_specs=(rows, rows, rows, P(), P(), P()), out_specs=rows, check_vma=False)
```

```python
import functools

import jax
import jax.numpy as jnp
from jax import lax
from jax.experimental import pallas as pl
from jax.experimental.pallas import tpu as pltpu
from jax.sharding import Mesh
from jax.sharding import PartitionSpec as P

HEAD = 128
BLK = 128
MAXLEN = 7
HDR = 2
DEPTH = 4
GROUP = 8
WINDOW = MAXLEN - 1
NEAR = 2 * GROUP
SLOTS = GROUP * (DEPTH - 2) * HDR + HDR
FAST_SLOTS = 8
REST_SLOTS = SLOTS - FAST_SLOTS
CHUNKS = 2
STACK = 8
LIST = WINDOW + (DEPTH - 1) * HDR
NEG = -1e30
VMEM_LIMIT = 48 * 1024 * 1024
EXP_SCALE = HEAD ** (-0.5) * 1.4426950408889634


def lookup(table, ids):
    slots = jnp.arange(table.shape[0], dtype=jnp.int32)
    return jnp.sum(jnp.where(ids[..., None] == slots, table, 0), axis=-1)


def tree_tables(lengths, parents, headers, group_id, groups, order, place):
    child = jnp.arange(lengths.shape[0], dtype=jnp.int32)
    before = child[None, :] < child[:, None]
    starts = jnp.sum(jnp.where(before, lengths[None, :], 0), axis=1)
    header_len = jnp.minimum(headers, lengths)

    ancestor = jnp.zeros(before.shape, bool)
    climbed = child
    for _ in range(DEPTH - 1):
        has_parent = climbed != 0
        climbed = lookup(parents, climbed)
        ancestor |= has_parent[:, None] & (climbed[:, None] == child[None, :])

    first = jnp.arange(groups, dtype=jnp.int32)[:, None] * GROUP
    present = (starts[None, :] < first + GROUP) & ((starts + lengths)[None, :] > first)
    needed = jnp.any(present[:, :, None] & ancestor[None, :, :], axis=1)
    count = jnp.where(needed, header_len[None, :], 0)
    slot_of = jnp.sum(jnp.where(before[None, :, :], count[:, None, :], 0), axis=2)
    most = jnp.max(jnp.sum(count, axis=1))
    slot = jnp.arange(SLOTS, dtype=jnp.int32)[None, :, None]
    offset = slot - slot_of[:, None, :]
    inside = (offset >= 0) & (offset < count[:, None, :])
    slot_block = jnp.sum(jnp.where(inside, starts[None, None, :] + offset, 0), axis=2)

    block = group_id * GROUP + order
    owner = jnp.sum((starts[None, :] <= block[:, None]).astype(jnp.int32), axis=1) - 1
    start = lookup(starts, owner)
    filled = block - start
    my_slots = lax.dynamic_index_in_dim(slot_of, group_id, 0, keepdims=False)
    k = jnp.arange(LIST, dtype=jnp.int32)[None, :]
    near = (start - group_id * GROUP + GROUP)[:, None] + k
    half = near // GROUP
    near = half * GROUP + place(near - half * GROUP)
    entries = jnp.where(k < filled[:, None], near, 0)
    current = owner
    for _ in range(DEPTH - 1):
        has_parent = current != 0
        current = lookup(parents, current)
        size = jnp.where(has_parent, lookup(header_len, current), 0)
        at = NEAR + lookup(my_slots, current)
        here = (k >= filled[:, None]) & (k < (filled + size)[:, None])
        entries = jnp.where(here, at[:, None] + k - filled[:, None], entries)
        filled = filled + size
    return slot_block, most, entries, filled


def attend_kernel(chunk, filled_ref, entries_ref, order_ref, *refs):
    near_and_far, query_refs, refs = refs[:4], refs[4:4 + GROUP], refs[4 + GROUP:]
    out_ref, pool, asked, sems, query_sems, scores, top, acc, den = refs
    step = pl.program_id(0)
    rows = top.shape[0]
    heads = rows // BLK
    width = heads * HEAD

    def query_copy(n):
        return pltpu.make_async_copy(
            query_refs[n].at[:, pl.ds(chunk * width, width)], asked.at[n], query_sems.at[n]
        )

    @pl.when(step == 0)
    def _():
        copies = []
        at = 0
        for n, ref in enumerate(near_and_far):
            copies.append(pltpu.make_async_copy(ref, pool.at[pl.ds(at, ref.shape[0])], sems.at[n]))
            at += ref.shape[0]
        query_copy(0).start()
        for c in copies:
            c.start()
        for n in range(1, GROUP):
            query_copy(n).start()
        for c in copies:
            c.wait()

    for n in range(GROUP):
        @pl.when(step == n)
        def _():
            query_copy(n).wait()

    filled = filled_ref[step]
    pairs = filled // 2
    odd = filled - 2 * pairs
    last = entries_ref[step, jnp.maximum(filled - 1, 0)]
    diagonal = GROUP + step

    def tile(which, a, b):
        return jnp.concatenate([pool[a, which], pool[b, which]], axis=0)

    def queries(g):
        return jnp.concatenate(
            [asked[step, :, h * HEAD:(h + 1) * HEAD] for h in range(g * STACK, (g + 1) * STACK)], axis=0
        )

    def score(q, keys):
        return lax.dot_general(q, keys, (((1,), (1,)), ((), ())), preferred_element_type=jnp.float32)

    tall = STACK * BLK
    groups = heads // STACK
    row = lax.broadcasted_iota(jnp.int32, (tall, 2 * BLK), 0) % BLK
    col = lax.broadcasted_iota(jnp.int32, (tall, 2 * BLK), 1)
    usable = (col <= row) | ((col >= BLK) & (odd == 1))
    keys = tile(0, diagonal, last)
    for g in range(groups):
        s = jnp.where(usable, score(queries(g), keys), NEG)
        r = slice(g * tall, (g + 1) * tall)
        scores[0, r, :] = s
        top[r, :] = jnp.maximum(s[:, :BLK], s[:, BLK:])

    def first_pass(p, carry):
        keys = tile(0, entries_ref[step, 2 * p], entries_ref[step, 2 * p + 1])
        for g in range(groups):
            s = score(queries(g), keys)
            r = slice(g * tall, (g + 1) * tall)
            scores[p + 1, r, :] = s
            top[r, :] = jnp.maximum(top[r, :], jnp.maximum(s[:, :BLK], s[:, BLK:]))
        return carry

    lax.fori_loop(0, pairs, first_pass, 0)

    def weigh(p, a, b, fresh):
        vals = tile(1, a, b)
        for g in range(groups):
            r = slice(g * tall, (g + 1) * tall)
            t = top[r, :]
            s = scores[p, r, :]
            w0 = jnp.exp2((s[:, :BLK] - t) * EXP_SCALE)
            w1 = jnp.exp2((s[:, BLK:] - t) * EXP_SCALE)
            mixed = jnp.dot(
                jnp.concatenate([w0, w1], axis=1).astype(jnp.bfloat16), vals,
                preferred_element_type=jnp.float32,
            )
            if fresh:
                den[r, :] = w0 + w1
                acc[r, :] = mixed
            else:
                den[r, :] += w0 + w1
                acc[r, :] += mixed

    for h in range(heads):
        r = slice(h * BLK, (h + 1) * BLK)
        top[r, :] = jnp.broadcast_to(jnp.max(top[r, :], axis=1, keepdims=True), (BLK, BLK))
    weigh(0, diagonal, last, True)

    def second_pass(p, carry):
        weigh(p + 1, entries_ref[step, 2 * p], entries_ref[step, 2 * p + 1], False)
        return carry

    lax.fori_loop(0, pairs, second_pass, 0)
    for h in range(heads):
        r = slice(h * BLK, (h + 1) * BLK)
        total = jnp.sum(den[r, :], axis=1, keepdims=True)
        out_ref[0, :, h * HEAD:(h + 1) * HEAD] = (acc[r, :] / total).astype(out_ref.dtype)


def pack_kernel(target_ref, query_ref, *refs):
    out_refs, (held, in_sems, out_sems) = refs[:GROUP], refs[GROUP:]
    width = held.shape[2]

    def fetch(n):
        at = pl.multiple_of(target_ref[n] * width, width)
        return pltpu.make_async_copy(query_ref.at[:, pl.ds(at, width)], held.at[n], in_sems.at[n])

    def put(n):
        return pltpu.make_async_copy(held.at[n], out_refs[n], out_sems.at[n])

    for n in range(GROUP):
        fetch(n).start()
    for n in range(GROUP):
        fetch(n).wait()
        put(n).start()
    for n in range(GROUP):
        put(n).wait()


def pack(targets, queries):
    total = queries.shape[1]
    width = total // GROUP
    return pl.pallas_call(
        pack_kernel,
        out_shape=[jax.ShapeDtypeStruct((BLK, width), queries.dtype)] * GROUP,
        in_specs=[pl.BlockSpec(memory_space=pltpu.SMEM), pl.BlockSpec(memory_space=pl.ANY)],
        out_specs=[pl.BlockSpec(memory_space=pl.ANY)] * GROUP,
        scratch_shapes=[
            pltpu.VMEM((GROUP, BLK, width), queries.dtype),
            pltpu.SemaphoreType.DMA((GROUP,)),
            pltpu.SemaphoreType.DMA((GROUP,)),
        ],
        cost_estimate=pl.CostEstimate(flops=0, bytes_accessed=4 * BLK * total, transcendentals=0),
        name="pack",
    )(targets, queries)


def unpack_kernel(chunk, part_ref, *refs):
    out_ref, held, in_sems, out_sems = refs[-4:]
    width = held.shape[2]

    def fetch(n):
        return pltpu.make_async_copy(part_ref.at[n], held.at[n], in_sems.at[n])

    def put(n):
        at = (n * CHUNKS + chunk) * width
        return pltpu.make_async_copy(held.at[n], out_ref.at[:, pl.ds(at, width)], out_sems.at[n])

    for n in range(GROUP):
        fetch(n).start()
    for n in range(GROUP):
        fetch(n).wait()
        put(n).start()
    for n in range(GROUP):
        put(n).wait()


def unpack(part, chunk, whole):
    width = part.shape[2]
    held = () if whole is None else (whole,)
    return pl.pallas_call(
        functools.partial(unpack_kernel, chunk),
        out_shape=jax.ShapeDtypeStruct((BLK, GROUP * CHUNKS * width), part.dtype),
        in_specs=[pl.BlockSpec(memory_space=pl.ANY)] * (1 + len(held)),
        out_specs=pl.BlockSpec(memory_space=pl.ANY),
        scratch_shapes=[
            pltpu.VMEM((GROUP, BLK, width), part.dtype),
            pltpu.SemaphoreType.DMA((GROUP,)),
            pltpu.SemaphoreType.DMA((GROUP,)),
        ],
        input_output_aliases={1: 0} if held else {},
        cost_estimate=pl.CostEstimate(
            flops=0, bytes_accessed=4 * BLK * GROUP * width, transcendentals=0
        ),
        name="unpack",
    )(part, *held)


def attend(filled, entries, order, before, own, fast, rest, query, chunk):
    width = query[0].shape[1] // CHUNKS
    rows = width // HEAD * BLK
    longest = 1 + LIST // 2
    return pl.pallas_call(
        functools.partial(attend_kernel, chunk),
        out_shape=jax.ShapeDtypeStruct((GROUP, BLK, width), query[0].dtype),
        grid_spec=pltpu.PrefetchScalarGridSpec(
            num_scalar_prefetch=3,
            grid=(GROUP,),
            in_specs=[pl.BlockSpec(memory_space=pl.ANY)] * (4 + GROUP),
            out_specs=pl.BlockSpec((1, BLK, width), lambda i, f, e, order_ref: (order_ref[i], 0, 0)),
            scratch_shapes=[
                pltpu.VMEM((NEAR + SLOTS, 2, BLK, HEAD), jnp.bfloat16),
                pltpu.VMEM((GROUP, BLK, width), jnp.bfloat16),
                pltpu.SemaphoreType.DMA((4,)),
                pltpu.SemaphoreType.DMA((GROUP,)),
                pltpu.VMEM((longest, rows, 2 * BLK), jnp.float32),
                pltpu.VMEM((rows, BLK), jnp.float32),
                pltpu.VMEM((rows, HEAD), jnp.float32),
                pltpu.VMEM((rows, BLK), jnp.float32),
            ],
        ),
        compiler_params=pltpu.CompilerParams(vmem_limit_bytes=VMEM_LIMIT),
        cost_estimate=pl.CostEstimate(
            flops=GROUP * rows * 4 * 8 * BLK * HEAD, bytes_accessed=6 << 20, transcendentals=0
        ),
        name="attend",
    )(filled, entries, order, before, own, fast, rest, *query)


def body(queries, keys, values, lengths, parents, headers):
    inside = ("c", "t")
    across = ("x", "z")
    group_id = lax.axis_index(across)
    groups = lax.axis_size(across)
    pieces = 2 * BLK // groups

    def tiles(a):
        return jnp.transpose(a.reshape(-1, pieces, GROUP, HEAD), (0, 2, 1, 3))

    def exchange(a):
        return lax.all_to_all(a, inside, split_axis=0, concat_axis=0, tiled=True)

    sent = jnp.concatenate([tiles(keys), tiles(values)], axis=0)
    everyone = lax.all_to_all(
        sent.reshape(-1, pieces, HEAD), across + inside, split_axis=0, concat_axis=0, tiled=True
    )
    core = lax.axis_index("c")
    ring = lax.axis_index("t")
    ring_size = lax.axis_size("t")
    core_size = lax.axis_size("c")
    moves = [(dc, dt) for dt in range(ring_size) for dc in range(core_size)]

    def place(r):
        return (ring - r % ring_size) % ring_size * core_size + (core ^ (r // ring_size))

    def move(piece, dc, dt):
        pairs = [
            (c * ring_size + t, (c ^ dc) * ring_size + (t + dt) % ring_size)
            for c in range(core_size)
            for t in range(ring_size)
        ]
        return lax.ppermute(piece, inside, pairs)

    def indices(sign):
        return jnp.stack([(core ^ dc) * ring_size + (ring + sign * dt) % ring_size for dc, dt in moves])

    targets = indices(1)
    order = indices(-1)
    packed = pack(targets, queries)
    mine = []
    for n, (dc, dt) in enumerate(moves):
        piece = packed[n]
        hop = 1 - 2 * dc
        if dt == 2:
            piece = move(piece, 0, hop)
        elif dc or dt:
            piece = move(piece, dc, dt)
        if dt == 2:
            piece = move(piece, dc, hop)
        mine.append(piece)

    slot_block, most, entries, filled = tree_tables(lengths, parents, headers, group_id, groups, order, place)
    blocks = (-1, 2, BLK, HEAD)
    own = []
    kept = lax.dynamic_slice_in_dim(sent, core * ring_size, ring_size, 1)
    given = lax.dynamic_slice_in_dim(sent, (1 - core) * ring_size, ring_size, 1)
    both = jnp.stack([kept, move(given, 1, 0)])
    for dt in range(ring_size):
        piece = lax.dynamic_index_in_dim(both, (ring + dt) % ring_size, 2, keepdims=False)
        own.append(move(piece, 0, dt) if dt else piece)
    own = jnp.stack(own).reshape(blocks)
    before = lax.ppermute(own, across, [(j, j + 1) for j in range(groups - 1)])

    def fetch(first, count):
        wanted = slot_block[:, first:first + count].reshape(-1)
        picked = jnp.take(everyone, wanted, axis=0, mode="clip").reshape(groups, count, pieces, HEAD)
        got = lax.all_to_all(picked, across, split_axis=0, concat_axis=0, tiled=True)
        return jnp.transpose(got, (1, 0, 2, 3)).reshape(blocks)

    fast = fetch(0, FAST_SLOTS)
    rest = lax.cond(
        most > FAST_SLOTS,
        lambda: fetch(FAST_SLOTS, REST_SLOTS),
        lambda: jnp.zeros((REST_SLOTS,) + own.shape[1:], own.dtype),
    )

    whole = None
    for chunk in range(CHUNKS):
        part = exchange(attend(filled, entries, order, before, own, fast, rest, mine, chunk))
        whole = unpack(part, chunk, whole)
    return whole


def solution(mesh):
    inner = Mesh(mesh.devices.reshape(4, 8, 2, 4), ("x", "z", "c", "t"))
    rows = P(("x", "z", "c", "t"), None)
    return jax.shard_map(
        body, mesh=inner, in_specs=(rows, rows, rows, P(), P(), P()), out_specs=rows, check_vma=False
    )
```

```python
import functools

import jax
import jax.numpy as jnp
from jax import lax
from jax.experimental import pallas as pl
from jax.experimental.pallas import tpu as pltpu
from jax.sharding import Mesh
from jax.sharding import PartitionSpec as P

HEAD = 128
BLK = 128
MAXLEN = 7
HDR = 2
DEPTH = 4
GROUP = 8
WINDOW = MAXLEN - 1
NEAR = 2 * GROUP
SLOTS = GROUP * (DEPTH - 2) * HDR + HDR
FAST_SLOTS = 8
REST_SLOTS = SLOTS - FAST_SLOTS
CHUNKS = 2
STACK = 1
LIST = WINDOW + (DEPTH - 1) * HDR
NEG = -1e30
VMEM_LIMIT = 48 * 1024 * 1024
EXP_SCALE = HEAD ** (-0.5) * 1.4426950408889634


def lookup(table, ids):
    slots = jnp.arange(table.shape[0], dtype=jnp.int32)
    return jnp.sum(jnp.where(ids[..., None] == slots, table, 0), axis=-1)


def tree_tables(lengths, parents, headers, group_id, groups, order, place):
    child = jnp.arange(lengths.shape[0], dtype=jnp.int32)
    before = child[None, :] < child[:, None]
    starts = jnp.sum(jnp.where(before, lengths[None, :], 0), axis=1)
    header_len = jnp.minimum(headers, lengths)

    ancestor = jnp.zeros(before.shape, bool)
    climbed = child
    for _ in range(DEPTH - 1):
        has_parent = climbed != 0
        climbed = lookup(parents, climbed)
        ancestor |= has_parent[:, None] & (climbed[:, None] == child[None, :])

    first = jnp.arange(groups, dtype=jnp.int32)[:, None] * GROUP
    present = (starts[None, :] < first + GROUP) & ((starts + lengths)[None, :] > first)
    needed = jnp.any(present[:, :, None] & ancestor[None, :, :], axis=1)
    count = jnp.where(needed, header_len[None, :], 0)
    slot_of = jnp.sum(jnp.where(before[None, :, :], count[:, None, :], 0), axis=2)
    most = jnp.max(jnp.sum(count, axis=1))
    slot = jnp.arange(SLOTS, dtype=jnp.int32)[None, :, None]
    offset = slot - slot_of[:, None, :]
    inside = (offset >= 0) & (offset < count[:, None, :])
    slot_block = jnp.sum(jnp.where(inside, starts[None, None, :] + offset, 0), axis=2)

    block = group_id * GROUP + order
    owner = jnp.sum((starts[None, :] <= block[:, None]).astype(jnp.int32), axis=1) - 1
    start = lookup(starts, owner)
    filled = block - start
    my_slots = lax.dynamic_index_in_dim(slot_of, group_id, 0, keepdims=False)
    k = jnp.arange(LIST, dtype=jnp.int32)[None, :]
    near = (start - group_id * GROUP + GROUP)[:, None] + k
    half = near // GROUP
    near = half * GROUP + place(near - half * GROUP)
    entries = jnp.where(k < filled[:, None], near, 0)
    current = owner
    for _ in range(DEPTH - 1):
        has_parent = current != 0
        current = lookup(parents, current)
        size = jnp.where(has_parent, lookup(header_len, current), 0)
        at = NEAR + lookup(my_slots, current)
        here = (k >= filled[:, None]) & (k < (filled + size)[:, None])
        entries = jnp.where(here, at[:, None] + k - filled[:, None], entries)
        filled = filled + size
    return slot_block, most, entries, filled


def attend_kernel(chunk, filled_ref, entries_ref, order_ref, *refs):
    near_and_far, query_refs, refs = refs[:4], refs[4:4 + GROUP], refs[4 + GROUP:]
    out_ref, pool, asked, sems, query_sems, scores, top, acc, den = refs
    step = pl.program_id(0)
    rows = top.shape[0]
    heads = rows // BLK
    width = heads * HEAD

    def query_copy(n):
        return pltpu.make_async_copy(
            query_refs[n].at[:, pl.ds(chunk * width, width)], asked.at[n], query_sems.at[n]
        )

    @pl.when(step == 0)
    def _():
        copies = []
        at = 0
        for n, ref in enumerate(near_and_far):
            copies.append(pltpu.make_async_copy(ref, pool.at[pl.ds(at, ref.shape[0])], sems.at[n]))
            at += ref.shape[0]
        query_copy(0).start()
        for c in copies:
            c.start()
        for n in range(1, GROUP):
            query_copy(n).start()
        for c in copies:
            c.wait()

    for n in range(GROUP):
        @pl.when(step == n)
        def _():
            query_copy(n).wait()

    filled = filled_ref[step]
    pairs = filled // 2
    odd = filled - 2 * pairs
    last = entries_ref[step, jnp.maximum(filled - 1, 0)]
    diagonal = GROUP + step

    def tile(which, a, b):
        return jnp.concatenate([pool[a, which], pool[b, which]], axis=0)

    def queries(g):
        return jnp.concatenate(
            [asked[step, :, h * HEAD:(h + 1) * HEAD] for h in range(g * STACK, (g + 1) * STACK)], axis=0
        )

    def score(q, keys):
        return lax.dot_general(q, keys, (((1,), (1,)), ((), ())), preferred_element_type=jnp.float32)

    tall = STACK * BLK
    groups = heads // STACK
    row = lax.broadcasted_iota(jnp.int32, (tall, 2 * BLK), 0) % BLK
    col = lax.broadcasted_iota(jnp.int32, (tall, 2 * BLK), 1)
    usable = (col <= row) | ((col >= BLK) & (odd == 1))
    keys = tile(0, diagonal, last)
    for g in range(groups):
        s = jnp.where(usable, score(queries(g), keys), NEG)
        r = slice(g * tall, (g + 1) * tall)
        scores[0, r, :] = s
        top[r, :] = jnp.maximum(s[:, :BLK], s[:, BLK:])

    def first_pass(p, carry):
        keys = tile(0, entries_ref[step, 2 * p], entries_ref[step, 2 * p + 1])
        for g in range(groups):
            s = score(queries(g), keys)
            r = slice(g * tall, (g + 1) * tall)
            scores[p + 1, r, :] = s
            top[r, :] = jnp.maximum(top[r, :], jnp.maximum(s[:, :BLK], s[:, BLK:]))
        return carry

    lax.fori_loop(0, pairs, first_pass, 0)

    def weigh(p, a, b, fresh):
        vals = tile(1, a, b)
        for g in range(groups):
            r = slice(g * tall, (g + 1) * tall)
            t = top[r, :]
            s = scores[p, r, :]
            w0 = jnp.exp2((s[:, :BLK] - t) * EXP_SCALE)
            w1 = jnp.exp2((s[:, BLK:] - t) * EXP_SCALE)
            mixed = jnp.dot(
                jnp.concatenate([w0, w1], axis=1).astype(jnp.bfloat16), vals,
                preferred_element_type=jnp.float32,
            )
            if fresh:
                den[r, :] = w0 + w1
                acc[r, :] = mixed
            else:
                den[r, :] += w0 + w1
                acc[r, :] += mixed

    for h in range(heads):
        r = slice(h * BLK, (h + 1) * BLK)
        top[r, :] = jnp.broadcast_to(jnp.max(top[r, :], axis=1, keepdims=True), (BLK, BLK))
    weigh(0, diagonal, last, True)

    def second_pass(p, carry):
        weigh(p + 1, entries_ref[step, 2 * p], entries_ref[step, 2 * p + 1], False)
        return carry

    lax.fori_loop(0, pairs, second_pass, 0)
    for h in range(heads):
        r = slice(h * BLK, (h + 1) * BLK)
        total = jnp.sum(den[r, :], axis=1, keepdims=True)
        out_ref[0, :, h * HEAD:(h + 1) * HEAD] = (acc[r, :] / total).astype(out_ref.dtype)


def pack_kernel(target_ref, query_ref, *refs):
    out_refs, (held, in_sems, out_sems) = refs[:GROUP], refs[GROUP:]
    width = held.shape[2]

    def fetch(n):
        at = pl.multiple_of(target_ref[n] * width, width)
        return pltpu.make_async_copy(query_ref.at[:, pl.ds(at, width)], held.at[n], in_sems.at[n])

    def put(n):
        return pltpu.make_async_copy(held.at[n], out_refs[n], out_sems.at[n])

    for n in range(GROUP):
        fetch(n).start()
    for n in range(GROUP):
        fetch(n).wait()
        put(n).start()
    for n in range(GROUP):
        put(n).wait()


def pack(targets, queries):
    total = queries.shape[1]
    width = total // GROUP
    return pl.pallas_call(
        pack_kernel,
        out_shape=[jax.ShapeDtypeStruct((BLK, width), queries.dtype)] * GROUP,
        in_specs=[pl.BlockSpec(memory_space=pltpu.SMEM), pl.BlockSpec(memory_space=pl.ANY)],
        out_specs=[pl.BlockSpec(memory_space=pl.ANY)] * GROUP,
        scratch_shapes=[
            pltpu.VMEM((GROUP, BLK, width), queries.dtype),
            pltpu.SemaphoreType.DMA((GROUP,)),
            pltpu.SemaphoreType.DMA((GROUP,)),
        ],
        cost_estimate=pl.CostEstimate(flops=0, bytes_accessed=4 * BLK * total, transcendentals=0),
        name="pack",
    )(targets, queries)


def unpack_kernel(chunk, part_ref, *refs):
    out_ref, held, in_sems, out_sems = refs[-4:]
    width = held.shape[2]

    def fetch(n):
        return pltpu.make_async_copy(part_ref.at[n], held.at[n], in_sems.at[n])

    def put(n):
        at = (n * CHUNKS + chunk) * width
        return pltpu.make_async_copy(held.at[n], out_ref.at[:, pl.ds(at, width)], out_sems.at[n])

    for n in range(GROUP):
        fetch(n).start()
    for n in range(GROUP):
        fetch(n).wait()
        put(n).start()
    for n in range(GROUP):
        put(n).wait()


def unpack(part, chunk, whole):
    width = part.shape[2]
    held = () if whole is None else (whole,)
    return pl.pallas_call(
        functools.partial(unpack_kernel, chunk),
        out_shape=jax.ShapeDtypeStruct((BLK, GROUP * CHUNKS * width), part.dtype),
        in_specs=[pl.BlockSpec(memory_space=pl.ANY)] * (1 + len(held)),
        out_specs=pl.BlockSpec(memory_space=pl.ANY),
        scratch_shapes=[
            pltpu.VMEM((GROUP, BLK, width), part.dtype),
            pltpu.SemaphoreType.DMA((GROUP,)),
            pltpu.SemaphoreType.DMA((GROUP,)),
        ],
        input_output_aliases={1: 0} if held else {},
        cost_estimate=pl.CostEstimate(
            flops=0, bytes_accessed=4 * BLK * GROUP * width, transcendentals=0
        ),
        name="unpack",
    )(part, *held)


def attend(filled, entries, order, before, own, fast, rest, query, chunk):
    width = query[0].shape[1] // CHUNKS
    rows = width // HEAD * BLK
    longest = 1 + LIST // 2
    return pl.pallas_call(
        functools.partial(attend_kernel, chunk),
        out_shape=jax.ShapeDtypeStruct((GROUP, BLK, width), query[0].dtype),
        grid_spec=pltpu.PrefetchScalarGridSpec(
            num_scalar_prefetch=3,
            grid=(GROUP,),
            in_specs=[pl.BlockSpec(memory_space=pl.ANY)] * (4 + GROUP),
            out_specs=pl.BlockSpec((1, BLK, width), lambda i, f, e, order_ref: (order_ref[i], 0, 0)),
            scratch_shapes=[
                pltpu.VMEM((NEAR + SLOTS, 2, BLK, HEAD), jnp.bfloat16),
                pltpu.VMEM((GROUP, BLK, width), jnp.bfloat16),
                pltpu.SemaphoreType.DMA((4,)),
                pltpu.SemaphoreType.DMA((GROUP,)),
                pltpu.VMEM((longest, rows, 2 * BLK), jnp.float32),
                pltpu.VMEM((rows, BLK), jnp.float32),
                pltpu.VMEM((rows, HEAD), jnp.float32),
                pltpu.VMEM((rows, BLK), jnp.float32),
            ],
        ),
        compiler_params=pltpu.CompilerParams(vmem_limit_bytes=VMEM_LIMIT),
        cost_estimate=pl.CostEstimate(
            flops=GROUP * rows * 4 * 8 * BLK * HEAD, bytes_accessed=6 << 20, transcendentals=0
        ),
        name="attend",
    )(filled, entries, order, before, own, fast, rest, *query)


def body(queries, keys, values, lengths, parents, headers):
    inside = ("c", "t")
    across = ("x", "z")
    group_id = lax.axis_index(across)
    groups = lax.axis_size(across)
    pieces = 2 * BLK // groups

    def tiles(a):
        return jnp.transpose(a.reshape(-1, pieces, GROUP, HEAD), (0, 2, 1, 3))

    def exchange(a):
        return lax.all_to_all(a, inside, split_axis=0, concat_axis=0, tiled=True)

    core = lax.axis_index("c")
    ring = lax.axis_index("t")
    ring_size = lax.axis_size("t")
    core_size = lax.axis_size("c")
    moves = [(dc, dt) for dt in range(ring_size) for dc in range(core_size)]

    def place(r):
        return (ring - r % ring_size) % ring_size * core_size + (core ^ (r // ring_size))

    def move(piece, dc, dt):
        pairs = [
            (c * ring_size + t, (c ^ dc) * ring_size + (t + dt) % ring_size)
            for c in range(core_size)
            for t in range(ring_size)
        ]
        return lax.ppermute(piece, inside, pairs)

    def indices(sign):
        return jnp.stack([(core ^ dc) * ring_size + (ring + sign * dt) % ring_size for dc, dt in moves])

    targets = indices(1)
    order = indices(-1)
    blocks = (-1, 2, BLK, HEAD)

    def split(pieces_of):
        kept = lax.dynamic_slice_in_dim(pieces_of, core * ring_size, ring_size, 1)
        given = lax.dynamic_slice_in_dim(pieces_of, (1 - core) * ring_size, ring_size, 1)
        taken = move(given, 1, 0)
        both = jnp.stack([kept, taken])
        got = []
        for dt in range(ring_size):
            piece = lax.dynamic_index_in_dim(both, (ring + dt) % ring_size, 2, keepdims=False)
            if dt:
                piece = move(piece, 0, dt)
            got.append(piece)
        return jnp.concatenate(got, axis=0)

    sent = jnp.concatenate([tiles(keys), tiles(values)], axis=0)
    shifted = lax.ppermute(sent, across, [(j, j + 1) for j in range(groups - 1)])
    near = split(sent)
    own = near.reshape(blocks)
    everyone = lax.all_to_all(
        jnp.transpose(near, (1, 0, 2, 3)), across, split_axis=0, concat_axis=0, tiled=True
    )
    everyone = everyone.reshape(-1, pieces, HEAD)
    before = split(shifted).reshape(blocks)

    packed = pack(targets, queries)
    mine = []
    for n, (dc, dt) in enumerate(moves):
        piece = packed[n]
        hop = 1 - 2 * dc
        if dt == 2:
            piece = move(piece, 0, hop)
        elif dc or dt:
            piece = move(piece, dc, dt)
        if dt == 2:
            piece = move(piece, dc, hop)
        mine.append(piece)

    slot_block, most, entries, filled = tree_tables(lengths, parents, headers, group_id, groups, order, place)

    def fetch(first, count):
        wanted = slot_block[:, first:first + count].reshape(-1)
        wanted = wanted // GROUP * GROUP + place(wanted % GROUP)
        picked = jnp.take(everyone, wanted, axis=0, mode="clip").reshape(groups, count, pieces, HEAD)
        got = lax.all_to_all(picked, across, split_axis=0, concat_axis=0, tiled=True)
        return jnp.transpose(got, (1, 0, 2, 3)).reshape(blocks)

    fast = fetch(0, FAST_SLOTS)
    rest = lax.cond(
        most > FAST_SLOTS,
        lambda: fetch(FAST_SLOTS, REST_SLOTS),
        lambda: jnp.zeros((REST_SLOTS,) + own.shape[1:], own.dtype),
    )

    whole = None
    for chunk in range(CHUNKS):
        part = exchange(attend(filled, entries, order, before, own, fast, rest, mine, chunk))
        whole = unpack(part, chunk, whole)
    return whole


def solution(mesh):
    inner = Mesh(mesh.devices.reshape(4, 8, 2, 4), ("x", "z", "c", "t"))
    rows = P(("x", "z", "c", "t"), None)
    return jax.shard_map(
        body, mesh=inner, in_specs=(rows, rows, rows, P(), P(), P()), out_specs=rows, check_vma=False
    )
```

```python
import functools

import jax
import jax.numpy as jnp
from jax import lax
from jax.experimental import pallas as pl
from jax.experimental.pallas import tpu as pltpu
from jax.sharding import Mesh
from jax.sharding import PartitionSpec as P

HEAD = 128
BLK = 128
MAXLEN = 7
HDR = 2
DEPTH = 4
GROUP = 8
WINDOW = MAXLEN - 1
NEAR = 2 * GROUP
SLOTS = GROUP * (DEPTH - 2) * HDR + HDR
FAST_SLOTS = 8
REST_SLOTS = SLOTS - FAST_SLOTS
CHUNK_HEADS = (4, 6, 6)
STACK = 2
LIST = WINDOW + (DEPTH - 1) * HDR
NEG = -1e30
VMEM_LIMIT = 48 * 1024 * 1024
EXP_SCALE = HEAD ** (-0.5) * 1.4426950408889634


def lookup(table, ids):
    slots = jnp.arange(table.shape[0], dtype=jnp.int32)
    return jnp.sum(jnp.where(ids[..., None] == slots, table, 0), axis=-1)


def tree_tables(lengths, parents, headers, group_id, groups, order, place):
    child = jnp.arange(lengths.shape[0], dtype=jnp.int32)
    before = child[None, :] < child[:, None]
    starts = jnp.sum(jnp.where(before, lengths[None, :], 0), axis=1)
    header_len = jnp.minimum(headers, lengths)

    ancestor = jnp.zeros(before.shape, bool)
    climbed = child
    for _ in range(DEPTH - 1):
        has_parent = climbed != 0
        climbed = lookup(parents, climbed)
        ancestor |= has_parent[:, None] & (climbed[:, None] == child[None, :])

    first = jnp.arange(groups, dtype=jnp.int32)[:, None] * GROUP
    present = (starts[None, :] < first + GROUP) & ((starts + lengths)[None, :] > first)
    needed = jnp.any(present[:, :, None] & ancestor[None, :, :], axis=1)
    count = jnp.where(needed, header_len[None, :], 0)
    slot_of = jnp.sum(jnp.where(before[None, :, :], count[:, None, :], 0), axis=2)
    most = jnp.max(jnp.sum(count, axis=1))
    slot = jnp.arange(SLOTS, dtype=jnp.int32)[None, :, None]
    offset = slot - slot_of[:, None, :]
    inside = (offset >= 0) & (offset < count[:, None, :])
    slot_block = jnp.sum(jnp.where(inside, starts[None, None, :] + offset, 0), axis=2)

    block = group_id * GROUP + order
    owner = jnp.sum((starts[None, :] <= block[:, None]).astype(jnp.int32), axis=1) - 1
    start = lookup(starts, owner)
    filled = block - start
    my_slots = lax.dynamic_index_in_dim(slot_of, group_id, 0, keepdims=False)
    k = jnp.arange(LIST, dtype=jnp.int32)[None, :]
    near = (start - group_id * GROUP + GROUP)[:, None] + k
    half = near // GROUP
    near = half * GROUP + place(near - half * GROUP)
    entries = jnp.where(k < filled[:, None], near, 0)
    current = owner
    for _ in range(DEPTH - 1):
        has_parent = current != 0
        current = lookup(parents, current)
        size = jnp.where(has_parent, lookup(header_len, current), 0)
        at = NEAR + lookup(my_slots, current)
        here = (k >= filled[:, None]) & (k < (filled + size)[:, None])
        entries = jnp.where(here, at[:, None] + k - filled[:, None], entries)
        filled = filled + size
    return slot_block, most, entries, filled


def attend_kernel(first_head, filled_ref, entries_ref, order_ref, *refs):
    near_and_far, query_refs, refs = refs[:4], refs[4:4 + GROUP], refs[4 + GROUP:]
    out_ref, pool, asked, sems, query_sems, scores, top, acc, den = refs
    step = pl.program_id(0)
    rows = top.shape[0]
    heads = rows // BLK
    width = heads * HEAD

    def query_copy(n):
        return pltpu.make_async_copy(
            query_refs[n].at[:, pl.ds(first_head * HEAD, width)], asked.at[n], query_sems.at[n]
        )

    @pl.when(step == 0)
    def _():
        copies = []
        at = 0
        for n, ref in enumerate(near_and_far):
            copies.append(pltpu.make_async_copy(ref, pool.at[pl.ds(at, ref.shape[0])], sems.at[n]))
            at += ref.shape[0]
        query_copy(0).start()
        for c in copies:
            c.start()
        for n in range(1, GROUP):
            query_copy(n).start()
        for c in copies:
            c.wait()

    for n in range(GROUP):
        @pl.when(step == n)
        def _():
            query_copy(n).wait()

    filled = filled_ref[step]
    pairs = filled // 2
    odd = filled - 2 * pairs
    last = entries_ref[step, jnp.maximum(filled - 1, 0)]
    diagonal = GROUP + step

    def tile(which, a, b):
        return jnp.concatenate([pool[a, which], pool[b, which]], axis=0)

    tall = STACK * BLK
    stacks = heads // STACK

    def rows_of(g):
        return pl.ds(g * tall, tall)

    def score(g, keys):
        q = jnp.concatenate(
            [asked[step, :, pl.ds(h * HEAD, HEAD)] for h in range(g * STACK, (g + 1) * STACK)], axis=0
        )
        return lax.dot_general(q, keys, (((1,), (1,)), ((), ())), preferred_element_type=jnp.float32)

    row = lax.broadcasted_iota(jnp.int32, (BLK, 2 * BLK), 0)
    col = lax.broadcasted_iota(jnp.int32, (BLK, 2 * BLK), 1)
    usable = (col <= row) | ((col >= BLK) & (odd == 1))

    keys = tile(0, diagonal, last)
    for g in range(stacks):
        s = score(g, keys)
        s = jnp.concatenate(
            [jnp.where(usable, s[n * BLK:(n + 1) * BLK], NEG) for n in range(STACK)], axis=0
        )
        scores[0, rows_of(g), :] = s
        top[rows_of(g), :] = jnp.maximum(s[:, :BLK], s[:, BLK:])

    def first_pass(p, carry):
        keys = tile(0, entries_ref[step, 2 * p], entries_ref[step, 2 * p + 1])
        for g in range(stacks):
            r = rows_of(g)
            s = score(g, keys)
            scores[p + 1, r, :] = s
            top[r, :] = jnp.maximum(top[r, :], jnp.maximum(s[:, :BLK], s[:, BLK:]))
        return carry

    lax.fori_loop(0, pairs, first_pass, 0)

    def weigh(p, a, b, fresh):
        vals = tile(1, a, b)
        for g in range(stacks):
            r = rows_of(g)
            t = top[r, :]
            s = scores[p, r, :]
            w0 = jnp.exp2((s[:, :BLK] - t) * EXP_SCALE)
            w1 = jnp.exp2((s[:, BLK:] - t) * EXP_SCALE)
            mixed = jnp.dot(
                jnp.concatenate([w0, w1], axis=1).astype(jnp.bfloat16), vals,
                preferred_element_type=jnp.float32,
            )
            if fresh:
                den[r, :] = w0 + w1
                acc[r, :] = mixed
            else:
                den[r, :] += w0 + w1
                acc[r, :] += mixed

    for g in range(stacks):
        r = rows_of(g)
        top[r, :] = jnp.broadcast_to(jnp.max(top[r, :], axis=1, keepdims=True), (tall, BLK))
    weigh(0, diagonal, last, True)

    def second_pass(p, carry):
        weigh(p + 1, entries_ref[step, 2 * p], entries_ref[step, 2 * p + 1], False)
        return carry

    lax.fori_loop(0, pairs, second_pass, 0)
    for h in range(heads):
        r = slice(h * BLK, (h + 1) * BLK)
        total = jnp.sum(den[r, :], axis=1, keepdims=True)
        out_ref[0, :, h * HEAD:(h + 1) * HEAD] = (acc[r, :] / total).astype(out_ref.dtype)


def pack_kernel(target_ref, query_ref, *refs):
    out_refs, (held, in_sems, out_sems) = refs[:GROUP], refs[GROUP:]
    width = held.shape[2]

    def fetch(n):
        at = pl.multiple_of(target_ref[n] * width, width)
        return pltpu.make_async_copy(query_ref.at[:, pl.ds(at, width)], held.at[n], in_sems.at[n])

    def put(n):
        return pltpu.make_async_copy(held.at[n], out_refs[n], out_sems.at[n])

    for n in range(GROUP):
        fetch(n).start()
    for n in range(GROUP):
        fetch(n).wait()
        put(n).start()
    for n in range(GROUP):
        put(n).wait()


def pack(targets, queries):
    total = queries.shape[1]
    width = total // GROUP
    return pl.pallas_call(
        pack_kernel,
        out_shape=[jax.ShapeDtypeStruct((BLK, width), queries.dtype)] * GROUP,
        in_specs=[pl.BlockSpec(memory_space=pltpu.SMEM), pl.BlockSpec(memory_space=pl.ANY)],
        out_specs=[pl.BlockSpec(memory_space=pl.ANY)] * GROUP,
        scratch_shapes=[
            pltpu.VMEM((GROUP, BLK, width), queries.dtype),
            pltpu.SemaphoreType.DMA((GROUP,)),
            pltpu.SemaphoreType.DMA((GROUP,)),
        ],
        cost_estimate=pl.CostEstimate(flops=0, bytes_accessed=4 * BLK * total, transcendentals=0),
        name="pack",
    )(targets, queries)


def unpack_kernel(first_head, stride, part_ref, *refs):
    out_ref, held, in_sems, out_sems = refs[-4:]
    width = held.shape[2]

    def fetch(n):
        return pltpu.make_async_copy(part_ref.at[n], held.at[n], in_sems.at[n])

    def put(n):
        at = n * stride + first_head * HEAD
        return pltpu.make_async_copy(held.at[n], out_ref.at[:, pl.ds(at, width)], out_sems.at[n])

    for n in range(GROUP):
        fetch(n).start()
    for n in range(GROUP):
        fetch(n).wait()
        put(n).start()
    for n in range(GROUP):
        put(n).wait()


def unpack(part, first_head, stride, whole):
    width = part.shape[2]
    held = () if whole is None else (whole,)
    return pl.pallas_call(
        functools.partial(unpack_kernel, first_head, stride),
        out_shape=jax.ShapeDtypeStruct((BLK, GROUP * stride), part.dtype),
        in_specs=[pl.BlockSpec(memory_space=pl.ANY)] * (1 + len(held)),
        out_specs=pl.BlockSpec(memory_space=pl.ANY),
        scratch_shapes=[
            pltpu.VMEM((GROUP, BLK, width), part.dtype),
            pltpu.SemaphoreType.DMA((GROUP,)),
            pltpu.SemaphoreType.DMA((GROUP,)),
        ],
        input_output_aliases={1: 0} if held else {},
        cost_estimate=pl.CostEstimate(
            flops=0, bytes_accessed=4 * BLK * GROUP * width, transcendentals=0
        ),
        name="unpack",
    )(part, *held)


def attend(filled, entries, order, before, own, fast, rest, query, first_head, heads):
    width = heads * HEAD
    rows = width // HEAD * BLK
    return pl.pallas_call(
        functools.partial(attend_kernel, first_head),
        out_shape=jax.ShapeDtypeStruct((GROUP, BLK, width), query[0].dtype),
        grid_spec=pltpu.PrefetchScalarGridSpec(
            num_scalar_prefetch=3,
            grid=(GROUP,),
            in_specs=[pl.BlockSpec(memory_space=pl.ANY)] * (4 + GROUP),
            out_specs=pl.BlockSpec((1, BLK, width), lambda i, f, e, order_ref: (order_ref[i], 0, 0)),
            scratch_shapes=[
                pltpu.VMEM((NEAR + SLOTS, 2, BLK, HEAD), jnp.bfloat16),
                pltpu.VMEM((GROUP, BLK, width), jnp.bfloat16),
                pltpu.SemaphoreType.DMA((4,)),
                pltpu.SemaphoreType.DMA((GROUP,)),
                pltpu.VMEM((1 + LIST // 2, rows, 2 * BLK), jnp.float32),
                pltpu.VMEM((rows, BLK), jnp.float32),
                pltpu.VMEM((rows, HEAD), jnp.float32),
                pltpu.VMEM((rows, BLK), jnp.float32),
            ],
        ),
        compiler_params=pltpu.CompilerParams(vmem_limit_bytes=VMEM_LIMIT),
        cost_estimate=pl.CostEstimate(
            flops=GROUP * rows * 4 * 8 * BLK * HEAD, bytes_accessed=6 << 20, transcendentals=0
        ),
        name="attend",
    )(filled, entries, order, before, own, fast, rest, *query)


def body(queries, keys, values, lengths, parents, headers):
    inside = ("c", "t")
    across = ("x", "z")
    group_id = lax.axis_index(across)
    groups = lax.axis_size(across)
    pieces = 2 * BLK // groups

    def tiles(a):
        return jnp.transpose(a.reshape(-1, pieces, GROUP, HEAD), (0, 2, 1, 3))

    def exchange(a):
        return lax.all_to_all(a, inside, split_axis=0, concat_axis=0, tiled=True)

    core = lax.axis_index("c")
    ring = lax.axis_index("t")
    ring_size = lax.axis_size("t")
    core_size = lax.axis_size("c")
    moves = [(dc, dt) for dt in range(ring_size) for dc in range(core_size)]

    def place(r):
        return (ring - r % ring_size) % ring_size * core_size + (core ^ (r // ring_size))

    def move(piece, dc, dt):
        pairs = [
            (c * ring_size + t, (c ^ dc) * ring_size + (t + dt) % ring_size)
            for c in range(core_size)
            for t in range(ring_size)
        ]
        return lax.ppermute(piece, inside, pairs)

    def indices(sign):
        return jnp.stack([(core ^ dc) * ring_size + (ring + sign * dt) % ring_size for dc, dt in moves])

    targets = indices(1)
    order = indices(-1)
    blocks = (-1, 2, BLK, HEAD)

    def split(pieces_of, late=()):
        kept = lax.dynamic_slice_in_dim(pieces_of, core * ring_size, ring_size, 1)
        given = lax.dynamic_slice_in_dim(pieces_of, (1 - core) * ring_size, ring_size, 1)
        taken = move(given, 1, 0)
        taken, *late = lax.optimization_barrier((taken, *late))
        both = jnp.stack([kept, taken])
        got = []
        for dt in range(ring_size):
            piece = lax.dynamic_index_in_dim(both, (ring + dt) % ring_size, 2, keepdims=False)
            if dt:
                piece = move(piece, 0, dt)
            got.append(piece)
        return jnp.concatenate(got, axis=0), late

    sent = jnp.concatenate([tiles(keys), tiles(values)], axis=0)
    shifted = lax.ppermute(sent, across, [(j, j + 1) for j in range(groups - 1)])
    near, _ = split(sent)
    own = near.reshape(blocks)
    everyone = lax.all_to_all(
        jnp.transpose(near, (1, 0, 2, 3)), across, split_axis=0, concat_axis=0, tiled=True
    )
    everyone = everyone.reshape(-1, pieces, HEAD)
    before, (lengths, parents, headers) = split(shifted, (lengths, parents, headers))
    before = before.reshape(blocks)

    packed = pack(targets, queries)
    mine = []
    for n, (dc, dt) in enumerate(moves):
        piece = packed[n]
        hop = 1 - 2 * dc
        if dt == 2:
            piece = move(piece, 0, hop)
        elif dc or dt:
            piece = move(piece, dc, dt)
        if dt == 2:
            piece = move(piece, dc, hop)
        mine.append(piece)

    slot_block, most, entries, filled = tree_tables(lengths, parents, headers, group_id, groups, order, place)

    def fetch(first, count):
        wanted = slot_block[:, first:first + count].reshape(-1)
        wanted = wanted // GROUP * GROUP + place(wanted % GROUP)
        picked = jnp.take(everyone, wanted, axis=0, mode="clip").reshape(groups, count, pieces, HEAD)
        got = lax.all_to_all(picked, across, split_axis=0, concat_axis=0, tiled=True)
        return jnp.transpose(got, (1, 0, 2, 3)).reshape(blocks)

    fast = fetch(0, FAST_SLOTS)
    rest = lax.cond(
        most > FAST_SLOTS,
        lambda: fetch(FAST_SLOTS, REST_SLOTS),
        lambda: jnp.zeros((REST_SLOTS,) + own.shape[1:], own.dtype),
    )

    whole = None
    first_head = 0
    for heads in CHUNK_HEADS:
        part = attend(filled, entries, order, before, own, fast, rest, mine, first_head, heads)
        part = exchange(part)
        whole = unpack(part, first_head, mine[0].shape[1], whole)
        first_head += heads
    return whole


def solution(mesh):
    inner = Mesh(mesh.devices.reshape(4, 8, 2, 4), ("x", "z", "c", "t"))
    rows = P(("x", "z", "c", "t"), None)
    return jax.shard_map(
        body, mesh=inner, in_specs=(rows, rows, rows, P(), P(), P()), out_specs=rows, check_vma=False
    )
```

```python
import functools

import jax
import jax.numpy as jnp
from jax import lax
from jax.experimental import pallas as pl
from jax.experimental.pallas import tpu as pltpu
from jax.sharding import Mesh
from jax.sharding import PartitionSpec as P

HEAD = 128
BLK = 128
MAXLEN = 7
HDR = 2
DEPTH = 4
GROUP = 8
WINDOW = MAXLEN - 1
NEAR = 2 * GROUP
SLOTS = GROUP * (DEPTH - 2) * HDR + HDR
FAST_SLOTS = 8
REST_SLOTS = SLOTS - FAST_SLOTS
CHUNK_HEADS = (8, 8)
STACK = 1
LIST = WINDOW + (DEPTH - 1) * HDR
NEG = -1e30
VMEM_LIMIT = 48 * 1024 * 1024
EXP_SCALE = HEAD ** (-0.5) * 1.4426950408889634


def lookup(table, ids):
    slots = jnp.arange(table.shape[0], dtype=jnp.int32)
    return jnp.sum(jnp.where(ids[..., None] == slots, table, 0), axis=-1)


def tree_tables(lengths, parents, headers, group_id, groups, order, place):
    child = jnp.arange(lengths.shape[0], dtype=jnp.int32)
    before = child[None, :] < child[:, None]
    starts = jnp.sum(jnp.where(before, lengths[None, :], 0), axis=1)
    header_len = jnp.minimum(headers, lengths)

    ancestor = jnp.zeros(before.shape, bool)
    climbed = child
    for _ in range(DEPTH - 1):
        has_parent = climbed != 0
        climbed = lookup(parents, climbed)
        ancestor |= has_parent[:, None] & (climbed[:, None] == child[None, :])

    first = jnp.arange(groups, dtype=jnp.int32)[:, None] * GROUP
    present = (starts[None, :] < first + GROUP) & ((starts + lengths)[None, :] > first)
    needed = jnp.any(present[:, :, None] & ancestor[None, :, :], axis=1)
    count = jnp.where(needed, header_len[None, :], 0)
    slot_of = jnp.sum(jnp.where(before[None, :, :], count[:, None, :], 0), axis=2)
    most = jnp.max(jnp.sum(count, axis=1))
    slot = jnp.arange(SLOTS, dtype=jnp.int32)[None, :, None]
    offset = slot - slot_of[:, None, :]
    inside = (offset >= 0) & (offset < count[:, None, :])
    slot_block = jnp.sum(jnp.where(inside, starts[None, None, :] + offset, 0), axis=2)

    block = group_id * GROUP + order
    owner = jnp.sum((starts[None, :] <= block[:, None]).astype(jnp.int32), axis=1) - 1
    start = lookup(starts, owner)
    filled = block - start
    my_slots = lax.dynamic_index_in_dim(slot_of, group_id, 0, keepdims=False)
    k = jnp.arange(LIST, dtype=jnp.int32)[None, :]
    near = (start - group_id * GROUP + GROUP)[:, None] + k
    half = near // GROUP
    near = half * GROUP + place(near - half * GROUP)
    entries = jnp.where(k < filled[:, None], near, 0)
    current = owner
    for _ in range(DEPTH - 1):
        has_parent = current != 0
        current = lookup(parents, current)
        size = jnp.where(has_parent, lookup(header_len, current), 0)
        at = NEAR + lookup(my_slots, current)
        here = (k >= filled[:, None]) & (k < (filled + size)[:, None])
        entries = jnp.where(here, at[:, None] + k - filled[:, None], entries)
        filled = filled + size
    return slot_block, most, entries, filled


def attend_kernel(first_head, filled_ref, entries_ref, order_ref, more_ref, *refs):
    near_and_far, query_refs, refs = refs[:4], refs[4:4 + GROUP], refs[4 + GROUP:]
    out_ref, pool, asked, sems, query_sems, scores, top, acc, den = refs
    step = pl.program_id(0)
    rows = top.shape[0]
    heads = rows // BLK
    width = heads * HEAD

    def query_copy(n):
        return pltpu.make_async_copy(
            query_refs[n].at[:, pl.ds(first_head * HEAD, width)], asked.at[n], query_sems.at[n]
        )

    @pl.when(step == 0)
    def _():
        copies = []
        at = 0
        for n, ref in enumerate(near_and_far[:3]):
            copies.append(pltpu.make_async_copy(ref, pool.at[pl.ds(at, ref.shape[0])], sems.at[n]))
            at += ref.shape[0]
        query_copy(0).start()
        for c in copies:
            c.start()
        for n in range(1, GROUP):
            query_copy(n).start()
        for c in copies:
            c.wait()

        @pl.when(more_ref[0] > 0)
        def _():
            rest_ref = near_and_far[3]
            rest_copy = pltpu.make_async_copy(rest_ref, pool.at[pl.ds(at, rest_ref.shape[0])], sems.at[3])
            rest_copy.start()
            rest_copy.wait()

    for n in range(GROUP):
        @pl.when(step == n)
        def _():
            query_copy(n).wait()

    filled = filled_ref[step]
    pairs = filled // 2
    odd = filled - 2 * pairs
    last = entries_ref[step, jnp.maximum(filled - 1, 0)]
    diagonal = GROUP + step

    def tile(which, a, b):
        return jnp.concatenate([pool[a, which], pool[b, which]], axis=0)

    tall = STACK * BLK
    stacks = heads // STACK

    def rows_of(g):
        return pl.ds(g * tall, tall)

    def score(g, keys):
        q = jnp.concatenate(
            [asked[step, :, pl.ds(h * HEAD, HEAD)] for h in range(g * STACK, (g + 1) * STACK)], axis=0
        )
        return lax.dot_general(q, keys, (((1,), (1,)), ((), ())), preferred_element_type=jnp.float32)

    row = lax.broadcasted_iota(jnp.int32, (BLK, 2 * BLK), 0)
    col = lax.broadcasted_iota(jnp.int32, (BLK, 2 * BLK), 1)
    usable = (col <= row) | ((col >= BLK) & (odd == 1))

    keys = tile(0, diagonal, last)
    for g in range(stacks):
        s = score(g, keys)
        s = jnp.concatenate(
            [jnp.where(usable, s[n * BLK:(n + 1) * BLK], NEG) for n in range(STACK)], axis=0
        )
        scores[0, rows_of(g), :] = s
        top[rows_of(g), :] = jnp.maximum(s[:, :BLK], s[:, BLK:])

    def first_pass(p, carry):
        keys = tile(0, entries_ref[step, 2 * p], entries_ref[step, 2 * p + 1])
        for g in range(stacks):
            r = rows_of(g)
            s = score(g, keys)
            scores[p + 1, r, :] = s
            top[r, :] = jnp.maximum(top[r, :], jnp.maximum(s[:, :BLK], s[:, BLK:]))
        return carry

    lax.fori_loop(0, pairs, first_pass, 0)

    def weigh(p, a, b, fresh):
        vals = tile(1, a, b)
        for g in range(stacks):
            r = rows_of(g)
            t = top[r, :]
            s = scores[p, r, :]
            w0 = jnp.exp2((s[:, :BLK] - t) * EXP_SCALE)
            w1 = jnp.exp2((s[:, BLK:] - t) * EXP_SCALE)
            mixed = jnp.dot(
                jnp.concatenate([w0, w1], axis=1).astype(jnp.bfloat16), vals,
                preferred_element_type=jnp.float32,
            )
            if fresh:
                den[r, :] = w0 + w1
                acc[r, :] = mixed
            else:
                den[r, :] += w0 + w1
                acc[r, :] += mixed

    for g in range(stacks):
        r = rows_of(g)
        top[r, :] = jnp.broadcast_to(jnp.max(top[r, :], axis=1, keepdims=True), (tall, BLK))
    weigh(0, diagonal, last, True)

    def second_pass(p, carry):
        weigh(p + 1, entries_ref[step, 2 * p], entries_ref[step, 2 * p + 1], False)
        return carry

    lax.fori_loop(0, pairs, second_pass, 0)
    for h in range(heads):
        r = slice(h * BLK, (h + 1) * BLK)
        total = jnp.sum(den[r, :], axis=1, keepdims=True)
        out_ref[0, :, h * HEAD:(h + 1) * HEAD] = (acc[r, :] / total).astype(out_ref.dtype)


def pack_kernel(target_ref, query_ref, *refs):
    out_refs, (held, in_sems, out_sems) = refs[:GROUP], refs[GROUP:]
    width = held.shape[2]

    def fetch(n):
        at = pl.multiple_of(target_ref[n] * width, width)
        return pltpu.make_async_copy(query_ref.at[:, pl.ds(at, width)], held.at[n], in_sems.at[n])

    def put(n):
        return pltpu.make_async_copy(held.at[n], out_refs[n], out_sems.at[n])

    for n in range(GROUP):
        fetch(n).start()
    for n in range(GROUP):
        fetch(n).wait()
        put(n).start()
    for n in range(GROUP):
        put(n).wait()


def pack(targets, queries):
    total = queries.shape[1]
    width = total // GROUP
    return pl.pallas_call(
        pack_kernel,
        out_shape=[jax.ShapeDtypeStruct((BLK, width), queries.dtype)] * GROUP,
        in_specs=[pl.BlockSpec(memory_space=pltpu.SMEM), pl.BlockSpec(memory_space=pl.ANY)],
        out_specs=[pl.BlockSpec(memory_space=pl.ANY)] * GROUP,
        scratch_shapes=[
            pltpu.VMEM((GROUP, BLK, width), queries.dtype),
            pltpu.SemaphoreType.DMA((GROUP,)),
            pltpu.SemaphoreType.DMA((GROUP,)),
        ],
        cost_estimate=pl.CostEstimate(flops=0, bytes_accessed=4 * BLK * total, transcendentals=0),
        name="pack",
    )(targets, queries)


def unpack_kernel(first_head, stride, part_ref, *refs):
    out_ref, held, in_sems, out_sems = refs[-4:]
    width = held.shape[2]

    def fetch(n):
        return pltpu.make_async_copy(part_ref.at[n], held.at[n], in_sems.at[n])

    def put(n):
        at = n * stride + first_head * HEAD
        return pltpu.make_async_copy(held.at[n], out_ref.at[:, pl.ds(at, width)], out_sems.at[n])

    for n in range(GROUP):
        fetch(n).start()
    for n in range(GROUP):
        fetch(n).wait()
        put(n).start()
    for n in range(GROUP):
        put(n).wait()


def unpack(part, first_head, stride, whole):
    width = part.shape[2]
    held = () if whole is None else (whole,)
    return pl.pallas_call(
        functools.partial(unpack_kernel, first_head, stride),
        out_shape=jax.ShapeDtypeStruct((BLK, GROUP * stride), part.dtype),
        in_specs=[pl.BlockSpec(memory_space=pl.ANY)] * (1 + len(held)),
        out_specs=pl.BlockSpec(memory_space=pl.ANY),
        scratch_shapes=[
            pltpu.VMEM((GROUP, BLK, width), part.dtype),
            pltpu.SemaphoreType.DMA((GROUP,)),
            pltpu.SemaphoreType.DMA((GROUP,)),
        ],
        input_output_aliases={1: 0} if held else {},
        cost_estimate=pl.CostEstimate(
            flops=0, bytes_accessed=4 * BLK * GROUP * width, transcendentals=0
        ),
        name="unpack",
    )(part, *held)


def attend(filled, entries, order, overflow, before, own, fast, rest, query, first_head, heads):
    width = heads * HEAD
    rows = width // HEAD * BLK
    return pl.pallas_call(
        functools.partial(attend_kernel, first_head),
        out_shape=jax.ShapeDtypeStruct((GROUP, BLK, width), query[0].dtype),
        grid_spec=pltpu.PrefetchScalarGridSpec(
            num_scalar_prefetch=4,
            grid=(GROUP,),
            in_specs=[pl.BlockSpec(memory_space=pl.ANY)] * (4 + GROUP),
            out_specs=pl.BlockSpec((1, BLK, width), lambda i, f, e, order_ref, m: (order_ref[i], 0, 0)),
            scratch_shapes=[
                pltpu.VMEM((NEAR + SLOTS, 2, BLK, HEAD), jnp.bfloat16),
                pltpu.VMEM((GROUP, BLK, width), jnp.bfloat16),
                pltpu.SemaphoreType.DMA((4,)),
                pltpu.SemaphoreType.DMA((GROUP,)),
                pltpu.VMEM((1 + LIST // 2, rows, 2 * BLK), jnp.float32),
                pltpu.VMEM((rows, BLK), jnp.float32),
                pltpu.VMEM((rows, HEAD), jnp.float32),
                pltpu.VMEM((rows, BLK), jnp.float32),
            ],
        ),
        compiler_params=pltpu.CompilerParams(vmem_limit_bytes=VMEM_LIMIT),
        cost_estimate=pl.CostEstimate(
            flops=GROUP * rows * 4 * 8 * BLK * HEAD, bytes_accessed=6 << 20, transcendentals=0
        ),
        name="attend",
    )(filled, entries, order, overflow, before, own, fast, rest, *query)


def body(queries, keys, values, lengths, parents, headers):
    inside = ("c", "t")
    across = ("x", "z")
    group_id = lax.axis_index(across)
    groups = lax.axis_size(across)
    pieces = 2 * BLK // groups

    def tiles(a):
        return jnp.transpose(a.reshape(-1, pieces, GROUP, HEAD), (0, 2, 1, 3))

    def exchange(a):
        return lax.all_to_all(a, inside, split_axis=0, concat_axis=0, tiled=True)

    core = lax.axis_index("c")
    ring = lax.axis_index("t")
    ring_size = lax.axis_size("t")
    core_size = lax.axis_size("c")
    moves = [(dc, dt) for dt in range(ring_size) for dc in range(core_size)]

    def place(r):
        return (ring - r % ring_size) % ring_size * core_size + (core ^ (r // ring_size))

    def move(piece, dc, dt):
        pairs = [
            (c * ring_size + t, (c ^ dc) * ring_size + (t + dt) % ring_size)
            for c in range(core_size)
            for t in range(ring_size)
        ]
        return lax.ppermute(piece, inside, pairs)

    def indices(sign):
        return jnp.stack([(core ^ dc) * ring_size + (ring + sign * dt) % ring_size for dc, dt in moves])

    targets = indices(1)
    order = indices(-1)
    blocks = (-1, 2, BLK, HEAD)

    def split(pieces_of, late=()):
        kept = lax.dynamic_slice_in_dim(pieces_of, core * ring_size, ring_size, 1)
        given = lax.dynamic_slice_in_dim(pieces_of, (1 - core) * ring_size, ring_size, 1)
        taken = move(given, 1, 0)
        taken, *late = lax.optimization_barrier((taken, *late))
        both = jnp.stack([kept, taken])
        got = []
        for dt in range(ring_size):
            piece = lax.dynamic_index_in_dim(both, (ring + dt) % ring_size, 2, keepdims=False)
            if dt:
                piece = move(piece, 0, dt)
            got.append(piece)
        return jnp.concatenate(got, axis=0), late

    sent = jnp.concatenate([tiles(keys), tiles(values)], axis=0)
    shifted = lax.ppermute(sent, across, [(j, j + 1) for j in range(groups - 1)])
    near, _ = split(sent)
    own = near.reshape(blocks)
    everyone = lax.all_to_all(
        jnp.transpose(near, (1, 0, 2, 3)), across, split_axis=0, concat_axis=0, tiled=True
    )
    everyone = everyone.reshape(-1, pieces, HEAD)
    before, (lengths, parents, headers) = split(shifted, (lengths, parents, headers))
    before = before.reshape(blocks)

    packed = pack(targets, queries)
    mine = []
    for n, (dc, dt) in enumerate(moves):
        piece = packed[n]
        hop = 1 - 2 * dc
        if dt == 2:
            piece = move(piece, 0, hop)
        elif dc or dt:
            piece = move(piece, dc, dt)
        if dt == 2:
            piece = move(piece, dc, hop)
        mine.append(piece)

    slot_block, most, entries, filled = tree_tables(lengths, parents, headers, group_id, groups, order, place)

    def fetch(first, count):
        wanted = slot_block[:, first:first + count].reshape(-1)
        wanted = wanted // GROUP * GROUP + place(wanted % GROUP)
        picked = jnp.take(everyone, wanted, axis=0, mode="clip").reshape(groups, count, pieces, HEAD)
        got = lax.all_to_all(picked, across, split_axis=0, concat_axis=0, tiled=True)
        return jnp.transpose(got, (1, 0, 2, 3)).reshape(blocks)

    fast = fetch(0, FAST_SLOTS)
    rest = lax.cond(
        most > FAST_SLOTS,
        lambda: fetch(FAST_SLOTS, REST_SLOTS),
        lambda: jnp.zeros((REST_SLOTS,) + own.shape[1:], own.dtype),
    )

    overflow = (most > FAST_SLOTS).astype(jnp.int32).reshape(1)
    whole = None
    first_head = 0
    for heads in CHUNK_HEADS:
        part = attend(filled, entries, order, overflow, before, own, fast, rest, mine, first_head, heads)
        part = exchange(part)
        whole = unpack(part, first_head, mine[0].shape[1], whole)
        first_head += heads
    return whole


def solution(mesh):
    inner = Mesh(mesh.devices.reshape(4, 8, 2, 4), ("x", "z", "c", "t"))
    rows = P(("x", "z", "c", "t"), None)
    return jax.shard_map(body, mesh=inner, in_specs=(rows, rows, rows, P(), P(), P()), out_specs=rows, check_vma=False)
```
